32 devices in a mesh: row: 8 (over z, x), col: 2 (over y), snode: 2 (over core).
Axes of the slice: x: 2, y: 2, z: 4, core: 2. Of those that a mesh axis runs over, the one named last changes fastest.
Arguments:
- ancestor_inverse: bfloat16 [40960, 20480], P(('snode', 'row'), 'col'), parts along dimension 0, may hold values from -8 to 8
- fill_mask: int32 [160, 80], P('snode'), parts along dimension 0, may hold values from 0 to 1, as said below
- block_order: int32 [4, 80], P('snode'), parts along dimension 0, may hold values from 0 to 79, each once within a row
- l_rows: bfloat16 [4, 20480, 256], P('snode', ('row', 'col')), parts along dimension 0, may hold values from -6 to 6
- diag_inverse: bfloat16 [4, 256, 256], P('snode'), parts along dimension 0, may hold values from -0.0024414062 to 0.0024414062
Outputs:
- ainv_kr: bfloat16 [4, 256, 20480], P('snode', None, ('row', 'col')), parts along dimension 0
The draws below stay inside these ranges and needn't reach their ends.
There are 2 independent parts, one for each index of `snode`. The reference program is written for one: setup_inputs(seed, part) draws one part's arguments, and reference() takes and returns one part's arrays. A program takes and returns all parts, laid end to end along the dimension named above; each array names one. Nothing has to cross between parts.
Inputs may be any that keep to these rules, and one draw needn't show every extreme that they name: Tile (i, j) takes part exactly where fill_mask is 1; diagonal tiles are always 1. `block_order`: each row is a permutation of the 80 ancestor blocks.
All inputs are finite; a program needn't handle non-finite values.
Results may differ from the reference program's by a relative error of at most 0.014.
Values may be sent and summed in bfloat16 or wider, within the bound.
A program may use at most 256 MiB of HBM per device.

```python
import jax
import jax.numpy as jnp
from jax import lax

TILE = 256
BLOCKS = 80
SNODES = 2
ORDER = 20480


def draw_fill_mask(key, part):
    sub_key = jax.random.fold_in(key, 11)
    row_ids = jnp.arange(BLOCKS, dtype=jnp.int32)[:, None]
    col_ids = jnp.arange(BLOCKS, dtype=jnp.int32)[None, :]
    threshold = 20 + 80 * row_ids // (BLOCKS - 1)
    drawn_value = jax.random.randint(sub_key, (BLOCKS, BLOCKS), 0, 100)
    filled = jnp.where(drawn_value < threshold, 1, 0)
    return jnp.where(row_ids == col_ids, 1, filled).astype(jnp.int32)


def levels(rng, shape, split, smallest, top_value):
    factor_of = 1.0
    for position, blocks in split:
        heights = jax.random.uniform(jax.random.fold_in(jax.random.fold_in(rng, 6), position), (blocks,), jnp.float32, smallest / len(split), top_value / len(split))
        factor_of = factor_of * jnp.repeat(jnp.exp(heights), shape[position] // blocks).reshape((-1,) + (1,) * (len(shape) - 1 - position))
    return factor_of


def gaussian(stream_key, dims, width, reach, cuts=(), held_as=jnp.bfloat16):
    loudness = levels(stream_key, dims, cuts, -0.22, 0.18) if cuts else 1.0
    drawn = jax.random.normal(stream_key, dims, jnp.float32) * width * loudness
    return jnp.minimum(jnp.maximum(drawn, -reach), reach).astype(held_as)


def setup_inputs(seed: int = 0, part: int = 0) -> dict:
    keys = jax.random.split(jax.random.key(seed), 6)
    part_splits = jax.random.split(jax.random.fold_in(keys[5], part), 6)
    ancestor_inverse = gaussian(part_splits[0], (ORDER, ORDER), 1.3, 8.0, ((0, 8), (1, 2)))
    fill_mask = draw_fill_mask(jax.random.fold_in(jax.random.fold_in(keys[5], part), 71), part)
    block_order = jax.vmap(lambda own: jax.random.permutation(own, BLOCKS))(jax.random.split(part_splits[2], SNODES)).reshape((SNODES, BLOCKS)).astype(jnp.int32)
    l_rows = gaussian(part_splits[3], (SNODES, ORDER, TILE), 1.0, 6.0, ((1, 16),))
    diag_inverse = gaussian(part_splits[4], (SNODES, TILE, TILE), (BLOCKS * TILE * TILE) ** -0.5, 0.0024414062)
    return dict(ancestor_inverse=ancestor_inverse, fill_mask=fill_mask, block_order=block_order, l_rows=l_rows, diag_inverse=diag_inverse)


def reference(ancestor_inverse, fill_mask, block_order, l_rows, diag_inverse):
    snode_count = diag_inverse.shape[0]
    tile_size = diag_inverse.shape[1]
    block_count = fill_mask.shape[0]
    normed = jnp.einsum("sxy,syz->sxz", l_rows.astype(jnp.float32), diag_inverse.astype(jnp.float32), precision=lax.Precision.HIGHEST).astype(jnp.bfloat16)
    pieces = normed.reshape(snode_count, block_count, tile_size, tile_size).astype(jnp.float32)
    targets = jnp.arange(block_count, dtype=jnp.int32)
    selector = (block_order[:, None, :] == targets[None, :, None]).astype(jnp.float32)
    aligned = jnp.einsum("saq,sqxy->saxy", selector, pieces, precision=lax.Precision.HIGHEST)
    stacked = aligned.transpose(1, 2, 0, 3).reshape(block_count * tile_size, snode_count * tile_size)

    def one_row(block_id):
        row_slab = lax.dynamic_slice_in_dim(ancestor_inverse, block_id * tile_size, tile_size, 0).astype(jnp.float32)
        row_gate = jnp.repeat(lax.dynamic_slice_in_dim(fill_mask, block_id, 1, 0)[0].astype(jnp.float32), tile_size)
        return -jnp.dot(row_slab * row_gate[None, :], stacked, precision=lax.Precision.HIGHEST)

    product = lax.map(one_row, jnp.arange(block_count, dtype=jnp.int32))
    product = product.reshape(block_count * tile_size, snode_count, tile_size)
    return product.transpose(1, 2, 0).astype(jnp.bfloat16)
```

```python
import functools

import jax
import jax.numpy as jnp
from jax import lax
from jax.experimental import pallas as pl
from jax.experimental.pallas import tpu as pltpu
from jax.sharding import PartitionSpec as P

MESH = pl.DeviceIdType.MESH
LANES = 128
PARTS = 4


def sizes(row_size, snodes, tile, held, local_rows, local_cols):
    depth = row_size // 2
    halves = tile // LANES
    phases = snodes * halves
    blocks = local_cols // tile
    away = [blocks // 4] * phases
    away[0] = 0
    away[-1] = blocks // 10
    return dict(
        depth=depth,
        halves=halves,
        phases=phases,
        snodes=snodes,
        tile=tile,
        held=held,
        blocks=blocks,
        shares=local_rows // (2 * tile),
        away=away,
    )


def fused_kernel(
    cfg, inv_ref, mask_ref, a_ref, l_ref, d_ref, out_ref, *rest
):
    depth, halves, phases = cfg["depth"], cfg["halves"], cfg["phases"]
    snodes, tile, held = cfg["snodes"], cfg["tile"], cfg["held"]
    blocks, shares, away = cfg["blocks"], cfg["shares"], cfg["away"]
    lanes = rest[:phases]
    (
        theirs_ref,
        mine_ref,
        l_vm,
        d_vm,
        own_ref,
        pick_ref,
        cols_ref,
        give_ref,
        take_ref,
        res_ref,
        b_send,
        b_recv,
        c_send,
        c_recv,
        y_send,
        y_recv,
        x_send,
        x_recv,
        f_send,
        f_recv,
        o_send,
        o_recv,
        a_sem,
        m_sem,
        in_sem,
        out_sem,
    ) = rest[phases:]
    quarter = tile // PARTS
    plane = PARTS * held

    row = lax.axis_index("row")
    y = lax.axis_index("col")
    core = lax.axis_index("snode")
    z = row // 2
    x = row % 2
    me = x * 2 + y
    lane_x = (1 - x) * 2 + y
    lane_y = x * 2 + 1 - y
    lane_d = (1 - x) * 2 + 1 - y
    slot = (row * 2 + y) * held

    def at(zz, xx, yy):
        return (zz * 2 + xx, yy, core)

    sides = [(at(z, 1 - x, y), lane_x), (at(z, x, 1 - y), lane_y), (at(z, 1 - x, 1 - y), lane_d)]
    to_x, to_y = sides[0][0], sides[1][0]
    pair = at(z + 1 - 2 * (z % 2), x, y)
    reach = [dz for dz in (2, -2, 1, -1) if abs(dz) < depth]

    def exists(dz):
        return z + dz < depth if dz > 0 else z + dz >= 0

    inner = jnp.logical_and(z >= 1, z + 1 < depth)
    low = z * 2 < depth
    far = jnp.where(low, z + 2, z - 2)
    near = jnp.where(low, z - 1, z + 1)

    loads = []
    for s in range(snodes):
        loads.append(pltpu.make_async_copy(l_ref.at[s], l_vm.at[s], in_sem.at[s, 0]))
        loads.append(pltpu.make_async_copy(d_ref.at[s], d_vm.at[s], in_sem.at[s, 1]))
    for c in loads:
        c.start()

    def theirs_load(i):
        return pltpu.make_async_copy(
            a_ref.at[pl.ds(((1 - y) * shares + i) * tile, tile)],
            theirs_ref.at[pl.ds(i * tile, tile)],
            a_sem.at[i],
        )

    def mine_load(g):
        return pltpu.make_async_copy(
            a_ref.at[pl.ds((y * shares + g % shares) * tile, tile)],
            mine_ref.at[g % 2],
            m_sem.at[g % 2],
        )

    for i in range(shares):
        theirs_load(i).start()
    for g in range(2):
        mine_load(g).start()

    barrier = pltpu.get_barrier_semaphore()
    for dev, _ in sides:
        pl.semaphore_signal(barrier, inc=1, device_id=dev, device_id_type=MESH)
    for dz in reach:

        @pl.when(exists(dz))
        def _():
            pl.semaphore_signal(barrier, inc=1, device_id=at(z + dz, x, y), device_id_type=MESH)

    def normalize(p):
        s, h = p // halves, p % halves
        rows = jnp.dot(
            l_vm[s], d_vm[s, :, h * LANES : (h + 1) * LANES], preferred_element_type=jnp.float32
        ).astype(own_ref.dtype)
        own_ref[p] = rows.reshape(held, PARTS, quarter, LANES).transpose(1, 0, 2, 3)
        lanes[p][pl.ds(slot, held)] = own_ref[p, me]

    for c in loads[:2]:
        c.wait()
    normalize(0)

    @pl.when(inner)
    def _():
        pl.semaphore_wait(barrier, len(sides) + 3)

    @pl.when(jnp.logical_not(inner))
    def _():
        pl.semaphore_wait(barrier, len(sides) + min(2, depth - 1))

    pending = []

    def remote(src, dst, send, recv, dev):
        return pltpu.make_async_remote_copy(
            src_ref=src, dst_ref=dst, send_sem=send, recv_sem=recv, device_id=dev, device_id_type=MESH
        )

    def guarded(cond, fn):
        if cond is None:
            fn()
        else:
            pl.when(cond)(fn)

    def start(make, cond=None):
        guarded(cond, lambda: make().start())
        pending.append((make, cond))

    def b_copy(p, k):
        dev, lane = sides[k]
        return remote(
            own_ref.at[p, lane], lanes[p].at[pl.ds(slot, held)], b_send.at[p, k], b_recv.at[p, k], dev
        )

    def spread(p):
        for k in (2, 0, 1):
            start(lambda k=k: b_copy(p, k))

    def c_copy(p, source, target, index):
        span = pl.ds(source * plane, plane)
        return remote(
            lanes[p].at[span],
            lanes[p].at[span],
            c_send.at[p, index],
            c_recv.at[p, source],
            at(target, x, y),
        )

    def climb(p):
        for k in range(3):
            b_copy(p, k).wait_recv()
        for n, dz in enumerate(reach):
            start(lambda n=n, dz=dz: c_copy(p, z, z + dz, n), exists(dz))

    def relay(p):
        if depth < 4:
            return

        @pl.when(inner)
        def _():
            c_copy(p, far, near, len(reach)).wait_recv()

        start(lambda: c_copy(p, far, near, len(reach)), inner)

    def climbed(p):
        for k in range(1, depth):
            source = (z + k) % depth
            cond = None
            if depth >= 4:
                cond = jnp.logical_not(jnp.logical_and(inner, source == far))
            guarded(cond, lambda: c_copy(p, source, z, 0).wait_recv())

    def y_copy(p):
        return remote(pick_ref.at[p], cols_ref.at[p, me], y_send.at[p], y_recv.at[p], to_y)

    def x_copy(p, k):
        lane = (me, lane_y)[k]
        span = pl.ds((z % 2) * away[p], blocks - away[p])
        return remote(
            cols_ref.at[p, lane, span],
            cols_ref.at[p, lane, span],
            x_send.at[p, k],
            x_recv.at[p, k],
            to_x,
        )

    def f_copy(p, k):
        lane = (lane_x, lane_d)[k]
        span = pl.ds((z % 2) * (blocks - away[p]), away[p])
        return remote(
            cols_ref.at[p, lane, span],
            cols_ref.at[p, lane, span],
            f_send.at[p, k],
            f_recv.at[p, k],
            pair,
        )

    def sort(p):
        climbed(p)
        s = p // halves

        def pick(j, carry):
            pick_ref[p, j] = lanes[p][inv_ref[s, (1 - y) * blocks + j]]
            cols_ref[p, me, j] = lanes[p][inv_ref[s, y * blocks + j]]
            return carry

        lax.fori_loop(0, blocks, pick, 0)
        start(lambda: y_copy(p))
        start(lambda: x_copy(p, 0))

    def pass_on(p):
        y_copy(p).wait_recv()
        start(lambda: x_copy(p, 1))

    def crossed(p):
        for k in range(2):
            x_copy(p, k).wait_recv()
            if away[p]:
                start(lambda k=k: f_copy(p, k))

    def forwarded(p):
        if away[p]:
            for k in range(2):
                f_copy(p, k).wait_recv()

    def gate_of(i, j):
        return mask_ref[i, y * blocks + j].astype(jnp.float32).astype(theirs_ref.dtype)

    def gate_theirs():
        first = row * 2 * shares + (1 - y) * shares

        def one_row(i, carry):
            pltpu.make_async_copy(
                a_ref.at[pl.ds(0, tile)], theirs_ref.at[pl.ds(i * tile, tile)], a_sem.at[i]
            ).wait()
            rows = pl.ds(pl.multiple_of(i * tile, tile), tile)

            def one(j, carry):
                span = pl.ds(pl.multiple_of(j * tile, tile), tile)
                theirs_ref[rows, span] = theirs_ref[rows, span] * gate_of(first + i, j)
                return carry

            return lax.fori_loop(0, blocks, one, carry)

        lax.fori_loop(0, shares, one_row, 0)

    step = max(n for n in range(1, 5) if blocks % n == 0)

    def columns(p, c):
        part = cols_ref[p, :, c * step : (c + 1) * step]
        return part.transpose(1, 0, 2, 3).reshape(step * tile, LANES)

    def o_copy(p, i):
        return remote(give_ref.at[p, i], take_ref.at[p, i], o_send.at[p, i], o_recv.at[p, i], to_y)

    def theirs(p):
        def block(i, carry):
            rows = pl.ds(pl.multiple_of(i * tile, tile), tile)
            total = jnp.zeros((tile, LANES), jnp.float32)
            for c in range(blocks // step):
                total += jnp.dot(
                    theirs_ref[rows, c * step * tile : (c + 1) * step * tile],
                    columns(p, c),
                    preferred_element_type=jnp.float32,
                )
            give_ref[p, i] = (-total).T.astype(give_ref.dtype)
            o_copy(p, i).start()
            return carry

        lax.fori_loop(0, shares, block, 0)
        for i in range(shares):
            pending.append((lambda i=i: o_copy(p, i), None))

    def mine(s):
        first = row * 2 * shares + y * shares

        def block(i, carry):
            g = s * shares + i
            mine_load(g).wait()
            total = jnp.zeros((tile, tile), jnp.float32)
            for c in range(blocks // step):
                left = jnp.concatenate(
                    [
                        mine_ref[g % 2, :, j * tile : (j + 1) * tile] * gate_of(first + i, j)
                        for j in range(c * step, (c + 1) * step)
                    ],
                    axis=1,
                )
                right = jnp.concatenate(
                    [columns(s * halves + h, c) for h in range(halves)], axis=1
                )
                total += jnp.dot(left, right, preferred_element_type=jnp.float32)

            @pl.when(g + 2 < snodes * shares)
            def _():
                mine_load(g + 2).start()

            total = (-total).T
            rows = pl.ds(pl.multiple_of(i * tile, tile), tile)
            for h in range(halves):
                o_copy(s * halves + h, i).wait_recv()
                span = slice(h * LANES, (h + 1) * LANES)
                res_ref[s, span, rows] = (
                    total[span] + take_ref[s * halves + h, i].astype(jnp.float32)
                ).astype(res_ref.dtype)
            return carry

        lax.fori_loop(0, shares, block, 0)
        pltpu.make_async_copy(res_ref.at[s], out_ref.at[s], out_sem.at[s]).start()

    spread(0)
    for c in loads[2:]:
        c.wait()
    for p in range(1, phases):
        normalize(p)
    for p in range(1, phases):
        spread(p)
    climb(0)
    gate_theirs()
    relay(0)
    climb(1)
    sort(0)
    for p in range(phases):
        if p + 1 < phases:
            relay(p + 1)
        if p + 2 < phases:
            climb(p + 2)
        pass_on(p)
        if p >= 1:
            forwarded(p - 1)
            theirs(p - 1)
            if p % halves == 0:
                mine(p // halves - 1)
        if p + 1 < phases:
            sort(p + 1)
        crossed(p)
    forwarded(phases - 1)
    theirs(phases - 1)
    mine(snodes - 1)
    for s in range(snodes):
        pltpu.make_async_copy(res_ref.at[s], out_ref.at[s], out_sem.at[s]).wait()
    for make, cond in pending:
        guarded(cond, lambda: make().wait_send())


def fused(inverse, mask, ancestor_inverse, l_rows, diag_inverse, row_size):
    local_rows, local_cols = ancestor_inverse.shape
    snodes, tile = diag_inverse.shape[:2]
    held = l_rows.shape[1] // tile
    cfg = sizes(row_size, snodes, tile, held, local_rows, local_cols)
    phases, blocks, shares, depth = cfg["phases"], cfg["blocks"], cfg["shares"], cfg["depth"]
    quarter = tile // PARTS
    total = inverse.shape[1]
    half = shares * tile
    kind = ancestor_inverse.dtype
    dma = pltpu.SemaphoreType.DMA
    scratch = [pltpu.VMEM((total, quarter, LANES), kind) for _ in range(phases)]
    scratch += [
        pltpu.VMEM((half, local_cols), kind),
        pltpu.VMEM((2, tile, local_cols), kind),
        pltpu.VMEM(l_rows.shape, kind),
        pltpu.VMEM(diag_inverse.shape, kind),
        pltpu.VMEM((phases, PARTS, held, quarter, LANES), kind),
        pltpu.VMEM((phases, blocks, quarter, LANES), kind),
        pltpu.VMEM((phases, PARTS, blocks, quarter, LANES), kind),
        pltpu.VMEM((phases, shares, LANES, tile), kind),
        pltpu.VMEM((phases, shares, LANES, tile), kind),
        pltpu.VMEM((snodes, tile, half), kind),
        dma((phases, 3)),
        dma((phases, 3)),
        dma((phases, 5)),
        dma((phases, depth)),
        dma((phases,)),
        dma((phases,)),
        dma((phases, 2)),
        dma((phases, 2)),
        dma((phases, 2)),
        dma((phases, 2)),
        dma((phases, shares)),
        dma((phases, shares)),
        dma((shares,)),
        dma((2,)),
        dma((snodes, 2)),
        dma((snodes,)),
    ]
    smem = pl.BlockSpec(memory_space=pltpu.SMEM)
    anywhere = pl.BlockSpec(memory_space=pl.ANY)
    return pl.pallas_call(
        functools.partial(fused_kernel, cfg),
        out_shape=jax.ShapeDtypeStruct((snodes, tile, half), kind),
        in_specs=[smem, smem, anywhere, anywhere, anywhere],
        out_specs=anywhere,
        scratch_shapes=scratch,
        compiler_params=pltpu.CompilerParams(
            collective_id=0, has_side_effects=True, vmem_limit_bytes=67043328
        ),
        name="fused",
    )(inverse, mask, ancestor_inverse, l_rows, diag_inverse)


def fast(ancestor_inverse, fill_mask, block_order, l_rows, diag_inverse):
    packed = jnp.arange(block_order.shape[1], dtype=jnp.int32)
    inverse = jnp.sum(
        jnp.where(block_order[:, None, :] == packed[None, :, None], packed[None, None, :], 0), axis=2
    ).astype(jnp.int32)
    return fused(
        inverse, fill_mask, ancestor_inverse, l_rows, diag_inverse, lax.axis_size("row")
    )


def plain(ancestor_inverse, fill_mask, block_order, l_rows, diag_inverse):
    row_index = lax.axis_index("row")
    col_index = lax.axis_index("col")
    local_rows, local_cols = ancestor_inverse.shape
    snode_count, tile_size = diag_inverse.shape[:2]
    block_count = fill_mask.shape[0]
    row_blocks = local_rows // tile_size
    col_blocks = local_cols // tile_size
    normed = jnp.einsum(
        "sxy,syz->sxz", l_rows, diag_inverse, preferred_element_type=jnp.float32
    ).astype(jnp.bfloat16)
    wanted = col_index * col_blocks + jnp.arange(col_blocks, dtype=jnp.int32)
    everything = lax.all_gather(normed, ("row", "col"), axis=1, tiled=True)
    pieces = everything.reshape(snode_count, block_count, tile_size, tile_size)
    selector = (block_order[:, None, :] == wanted[None, :, None]).astype(jnp.bfloat16)
    columns = jnp.einsum(
        "saq,sqxy->saxy", selector, pieces, preferred_element_type=jnp.float32
    ).astype(jnp.bfloat16)
    stacked = columns.transpose(1, 2, 0, 3).reshape(local_cols, snode_count * tile_size)
    tile_gate = lax.dynamic_slice(
        fill_mask, (row_index * row_blocks, col_index * col_blocks), (row_blocks, col_blocks)
    ).astype(jnp.bfloat16)
    masked = (
        ancestor_inverse.reshape(row_blocks, tile_size, col_blocks, tile_size)
        * tile_gate[:, None, :, None]
    ).reshape(local_rows, local_cols)
    share_rows = local_rows // lax.axis_size("col")
    own_rows = lax.psum_scatter(
        (-jnp.dot(masked, stacked, preferred_element_type=jnp.float32)).astype(jnp.bfloat16),
        "col",
        scatter_dimension=0,
        tiled=True,
    ).astype(jnp.float32)
    return (
        own_rows.reshape(share_rows, snode_count, tile_size).transpose(1, 2, 0).astype(jnp.bfloat16)
    )


def per_device(ancestor_inverse, fill_mask, block_order, l_rows, diag_inverse):
    tile = diag_inverse.shape[1]
    col_size = lax.axis_size("col")
    if (
        col_size == 2
        and lax.axis_size("row") in (4, 8)
        and tile % LANES == 0
        and tile % (PARTS * 16) == 0
        and l_rows.shape[1] % tile == 0
        and ancestor_inverse.shape[0] % (col_size * tile) == 0
    ):
        return fast(ancestor_inverse, fill_mask, block_order, l_rows, diag_inverse)
    return plain(ancestor_inverse, fill_mask, block_order, l_rows, diag_inverse)


def solution(mesh):
    return jax.shard_map(
        per_device,
        mesh=mesh,
        in_specs=(
            P(("snode", "row"), "col"),
            P("snode", None),
            P("snode", None),
            P("snode", ("row", "col"), None),
            P("snode", None, None),
        ),
        out_specs=P("snode", None, ("row", "col")),
        check_vma=False,
    )
```

```python
import functools

import jax
import jax.numpy as jnp
from jax import lax
from jax.experimental import pallas as pl
from jax.experimental.pallas import tpu as pltpu
from jax.sharding import PartitionSpec as P

MESH = pl.DeviceIdType.MESH
LANES = 128
PARTS = 4
AWAY = (0, 0, 0, 0, 14, 16, 18, 10)


def sizes(row_size, snodes, tile, held, local_rows, local_cols):
    blocks = local_cols // tile
    return dict(
        depth=row_size // 2,
        halves=tile // LANES,
        phases=2 * snodes * (tile // LANES),
        snodes=snodes,
        tile=tile,
        held=held,
        blocks=blocks,
        shares=local_rows // (2 * tile),
        away=[blocks * n // 40 for n in AWAY],
    )


def fused_kernel(cfg, inv_ref, mask_ref, a_ref, l_ref, d_ref, out_ref, *rest):
    depth, halves, phases = cfg["depth"], cfg["halves"], cfg["phases"]
    snodes, tile, held = cfg["snodes"], cfg["tile"], cfg["held"]
    blocks, shares, away = cfg["blocks"], cfg["shares"], cfg["away"]
    lanes, rest = rest[:phases], rest[phases:]
    cols, rest = rest[:phases], rest[phases:]
    (
        theirs_ref,
        mine_ref,
        l_vm,
        d_vm,
        own_ref,
        pick_ref,
        give_ref,
        take_ref,
        res_ref,
        part_ref,
        b_send,
        b_recv,
        c_send,
        c_recv,
        y_send,
        y_recv,
        x_send,
        x_recv,
        f_send,
        f_recv,
        o_send,
        o_recv,
        a_sem,
        m_sem,
        in_sem,
        out_sem,
    ) = rest
    strip = tile // PARTS // 2
    plane = PARTS * held
    final = phases // 2 - 1

    row = lax.axis_index("row")
    y = lax.axis_index("col")
    core = lax.axis_index("snode")
    z = row // 2
    x = row % 2
    me = x * 2 + y
    lane_x = (1 - x) * 2 + y
    lane_y = x * 2 + 1 - y
    lane_d = (1 - x) * 2 + 1 - y
    slot = (row * 2 + y) * held

    def at(zz, xx, yy):
        return (zz * 2 + xx, yy, core)

    sides = [(at(z, 1 - x, y), lane_x), (at(z, x, 1 - y), lane_y), (at(z, 1 - x, 1 - y), lane_d)]
    to_x, to_y = sides[0][0], sides[1][0]
    pair = at(z + 1 - 2 * (z % 2), x, y)
    reach = [dz for dz in (2, -2, 1, -1) if abs(dz) < depth]

    def exists(dz):
        return z + dz < depth if dz > 0 else z + dz >= 0

    inner = jnp.logical_and(z >= 1, z + 1 < depth)
    low = z * 2 < depth
    far = jnp.where(low, z + 2, z - 2)
    near = jnp.where(low, z - 1, z + 1)

    loads = []
    for s in range(snodes):
        loads.append(pltpu.make_async_copy(l_ref.at[s], l_vm.at[s], in_sem.at[s, 0]))
        loads.append(pltpu.make_async_copy(d_ref.at[s], d_vm.at[s], in_sem.at[s, 1]))
    for c in loads:
        c.start()

    def theirs_load(i):
        return pltpu.make_async_copy(
            a_ref.at[pl.ds(((1 - y) * shares + i) * tile, tile)],
            theirs_ref.at[pl.ds(i * tile, tile)],
            a_sem.at[i],
        )

    def mine_load(g):
        return pltpu.make_async_copy(
            a_ref.at[pl.ds((y * shares + g % shares) * tile, tile)],
            mine_ref.at[g % 2],
            m_sem.at[g % 2],
        )

    barrier = pltpu.get_barrier_semaphore()
    for dev, _ in sides:
        pl.semaphore_signal(barrier, inc=1, device_id=dev, device_id_type=MESH)
    for dz in reach:

        @pl.when(exists(dz))
        def _():
            pl.semaphore_signal(barrier, inc=1, device_id=at(z + dz, x, y), device_id_type=MESH)

    def normalize(g):
        s, h = g // halves, g % halves
        rows = jnp.dot(
            l_vm[s], d_vm[s, :, h * LANES : (h + 1) * LANES], preferred_element_type=jnp.float32
        ).reshape(held, PARTS, 2, strip, LANES)
        for u in range(2):
            own_ref[2 * g + u] = rows[:, :, u].astype(own_ref.dtype).transpose(1, 0, 2, 3)
            lanes[2 * g + u][pl.ds(slot, held)] = own_ref[2 * g + u, me]

    for c in loads[:2]:
        c.wait()
    normalize(0)

    @pl.when(inner)
    def _():
        pl.semaphore_wait(barrier, len(sides) + 3)

    @pl.when(jnp.logical_not(inner))
    def _():
        pl.semaphore_wait(barrier, len(sides) + min(2, depth - 1))

    pending = {}

    def remote(src, dst, send, recv, dev):
        return pltpu.make_async_remote_copy(
            src_ref=src, dst_ref=dst, send_sem=send, recv_sem=recv, device_id=dev, device_id_type=MESH
        )

    def guarded(cond, fn):
        if cond is None:
            fn()
        else:
            pl.when(cond)(fn)

    def start(key, make, cond=None):
        guarded(cond, lambda: make().start())
        pending.setdefault(key, []).append((make, cond))

    def drain(*key):
        for make, cond in pending.pop(key, []):
            guarded(cond, lambda make=make: make().wait_send())

    def b_copy(p, k):
        dev, lane = sides[k]
        return remote(
            own_ref.at[p, lane], lanes[p].at[pl.ds(slot, held)], b_send.at[p, k], b_recv.at[p, k], dev
        )

    def spread(p):
        for k in (2, 0, 1):
            start(("b", p), lambda k=k: b_copy(p, k))

    def c_copy(p, source, target, index):
        span = pl.ds(source * plane, plane)
        return remote(
            lanes[p].at[span],
            lanes[p].at[span],
            c_send.at[p, index],
            c_recv.at[p, source],
            at(target, x, y),
        )

    def climb(p):
        for k in range(3):
            b_copy(p, k).wait_recv()
        for n, dz in enumerate(reach):
            start(("c", p), lambda n=n, dz=dz: c_copy(p, z, z + dz, n), exists(dz))

    def relay(p):
        if depth < 4:
            return

        def c_far():
            return c_copy(p, far, near, len(reach))

        guarded(inner if p == phases - 1 else None, lambda: c_far().wait_recv())
        start(("c", p), c_far, inner)

    def climbed(p):
        for k in range(1, depth):
            source = (z + k) % depth
            cond = None
            if depth >= 4:
                cond = source != far
                if p == phases - 1:
                    cond = jnp.logical_or(cond, jnp.logical_not(inner))
            guarded(cond, lambda source=source: c_copy(p, source, z, 0).wait_recv())

    def y_copy(p):
        return remote(pick_ref.at[p], cols[p].at[me], y_send.at[p], y_recv.at[p], to_y)

    def pieces(p):
        first, rest = away[p], blocks - 2 * away[p]
        if not first:
            return [(0, 0, blocks)]
        return [(0, blocks - first, first)] + ([(first, first, rest)] if rest else [])

    def x_copy(p, k, n):
        lane = (me, lane_y)[k]
        even, odd, size = pieces(p)[n]
        span = pl.ds(even + (z % 2) * (odd - even), size)
        return remote(
            cols[p].at[lane, span], cols[p].at[lane, span], x_send.at[p, k, n], x_recv.at[p, k, n], to_x
        )

    def cross(p, k):
        for n in range(len(pieces(p))):
            start(("x", p), lambda n=n: x_copy(p, k, n))

    def f_copy(p, k):
        lane = (lane_x, lane_d)[k]
        span = pl.ds((z % 2) * (blocks - away[p]), away[p])
        return remote(
            cols[p].at[lane, span], cols[p].at[lane, span], f_send.at[p, k], f_recv.at[p, k], pair
        )

    def sort(p):
        climbed(p)
        s = p // (2 * halves)

        def pick(j, carry):
            pick_ref[p, j] = lanes[p][inv_ref[s, (1 - y) * blocks + j]]
            cols[p][me, j] = lanes[p][inv_ref[s, y * blocks + j]]
            return carry

        lax.fori_loop(0, blocks, pick, 0)
        start(("y", p), lambda: y_copy(p))
        cross(p, 0)

    def pass_on(p):
        y_copy(p).wait_recv()
        cross(p, 1)

    def forward(p, k):
        if away[p]:
            x_copy(p, k, 0).wait_recv()
            start(("f", p), lambda: f_copy(p, k))

    def crossed(p):
        for k in range(2):
            for n in range(1 if away[p] else 0, len(pieces(p))):
                x_copy(p, k, n).wait_recv()

    def forwarded(p):
        if away[p]:
            for k in range(2):
                f_copy(p, k).wait_recv()

    def gate_of(i, j):
        return mask_ref[i, y * blocks + j].astype(jnp.float32).astype(theirs_ref.dtype)

    def gate_theirs():
        first = row * 2 * shares + (1 - y) * shares

        def one_row(i, carry):
            pltpu.make_async_copy(
                a_ref.at[pl.ds(0, tile)], theirs_ref.at[pl.ds(i * tile, tile)], a_sem.at[i]
            ).wait()
            rows = pl.ds(pl.multiple_of(i * tile, tile), tile)

            def one(j, carry):
                span = pl.ds(pl.multiple_of(j * tile, tile), tile)
                theirs_ref[rows, span] = theirs_ref[rows, span] * gate_of(first + i, j)
                return carry

            return lax.fori_loop(0, blocks, one, carry)

        lax.fori_loop(0, shares, one_row, 0)

    step = max(n for n in range(1, 5) if blocks % n == 0)

    def stacked(strips):
        return jnp.stack(strips, axis=2).transpose(1, 0, 2, 3, 4).reshape(-1, LANES)

    def columns(g, c):
        js = slice(c * step, (c + 1) * step)
        return stacked([cols[2 * g + u][:, js] for u in range(2)])

    def o_copy(g, i):
        return remote(give_ref.at[g, i], take_ref.at[g, i], o_send.at[g, i], o_recv.at[g, i], to_y)

    def send_block(g, i, total):
        give_ref[g, i] = (-total).T.astype(give_ref.dtype)
        o_copy(g, i).start()

    def sent_blocks(g, lo, hi):
        for i in range(lo, hi):
            pending.setdefault(("o", g), []).append((lambda i=i: o_copy(g, i), None))

    def theirs(g, lo, hi):
        def block(i, carry):
            rows = pl.ds(pl.multiple_of(i * tile, tile), tile)
            total = jnp.zeros((tile, LANES), jnp.float32)
            for c in range(blocks // step):
                total += jnp.dot(
                    theirs_ref[rows, c * step * tile : (c + 1) * step * tile],
                    columns(g, c),
                    preferred_element_type=jnp.float32,
                )
            send_block(g, i, total)
            return carry

        lax.fori_loop(lo, hi, block, 0)
        sent_blocks(g, lo, hi)

    def theirs_half(g, last):
        side = 1 - x if last else x

        def block(i, carry):
            rows = pl.ds(pl.multiple_of(i * tile, tile), tile)
            total = jnp.zeros((tile, LANES), jnp.float32)
            for c in range(blocks // step):
                js = range(c * step, (c + 1) * step)
                left = jnp.concatenate(
                    [
                        theirs_ref[rows, pl.ds(pl.multiple_of(j * tile + side * LANES, LANES), LANES)]
                        for j in js
                    ],
                    axis=1,
                )
                right = [
                    cols[2 * g + u][pl.ds(side * 2, 2), c * step : (c + 1) * step] for u in range(2)
                ]
                total += jnp.dot(left, stacked(right), preferred_element_type=jnp.float32)
            if last:
                send_block(g, i, total + part_ref[rows])
            else:
                part_ref[rows] = total
            return carry

        lax.fori_loop(0, shares, block, 0)
        if last:
            sent_blocks(g, 0, shares)

    def mine(s, lo, hi):
        first = row * 2 * shares + y * shares

        def block(i, carry):
            n = s * shares + i
            mine_load(n).wait()
            total = jnp.zeros((tile, tile), jnp.float32)
            for c in range(blocks // step):
                left = jnp.concatenate(
                    [
                        mine_ref[n % 2, :, j * tile : (j + 1) * tile] * gate_of(first + i, j)
                        for j in range(c * step, (c + 1) * step)
                    ],
                    axis=1,
                )
                right = jnp.concatenate(
                    [columns(s * halves + h, c) for h in range(halves)], axis=1
                )
                total += jnp.dot(left, right, preferred_element_type=jnp.float32)

            @pl.when(n + 2 < snodes * shares)
            def _():
                mine_load(n + 2).start()

            total = (-total).T
            rows = pl.ds(pl.multiple_of(i * tile, tile), tile)
            for h in range(halves):
                o_copy(s * halves + h, i).wait_recv()
                span = slice(h * LANES, (h + 1) * LANES)
                res_ref[s, span, rows] = (
                    total[span] + take_ref[s * halves + h, i].astype(jnp.float32)
                ).astype(res_ref.dtype)
            return carry

        lax.fori_loop(lo, hi, block, 0)
        if hi == shares:
            pltpu.make_async_copy(res_ref.at[s], out_ref.at[s], out_sem.at[s]).start()

    spread(0)
    spread(1)
    for i in range(shares):
        theirs_load(i).start()
    for n in range(2):
        mine_load(n).start()
    for c in loads[2:]:
        c.wait()
    for g in range(1, phases // 2):
        normalize(g)
        spread(2 * g)
        spread(2 * g + 1)
    climb(0)
    gate_theirs()
    relay(0)
    climb(1)
    sort(0)
    relay(1)
    climb(2)
    pass_on(0)
    sort(1)
    relay(2)
    climb(3)
    pass_on(1)
    sort(2)
    relay(3)
    climb(4)
    crossed(0)
    crossed(1)
    pass_on(2)
    sort(3)
    theirs(0, 0, 3)
    relay(4)
    climb(5)
    theirs(0, 3, 5)
    pass_on(3)
    sort(4)
    relay(5)
    climb(6)
    crossed(2)
    pass_on(4)
    sort(5)
    relay(6)
    climb(7)
    crossed(3)
    theirs(1, 0, 3)
    pass_on(5)
    theirs(1, 3, 5)
    sort(6)
    relay(7)
    forward(4, 0)
    forward(4, 1)
    mine(0, 0, 3)
    pass_on(6)
    sort(7)
    forward(5, 0)
    mine(0, 3, 5)
    forward(5, 1)
    forward(6, 0)
    crossed(4)
    crossed(5)
    pass_on(7)
    forwarded(4)
    forwarded(5)
    theirs(2, 0, 3)
    forward(6, 1)
    theirs(2, 3, 5)
    forward(7, 0)
    theirs_half(final, False)
    forward(7, 1)
    crossed(6)
    crossed(7)
    forwarded(6)
    forwarded(7)
    theirs_half(final, True)
    mine(1, 0, 5)
    for s in range(snodes):
        pltpu.make_async_copy(res_ref.at[s], out_ref.at[s], out_sem.at[s]).wait()
    for key in list(pending):
        drain(*key)


def fused(inverse, mask, ancestor_inverse, l_rows, diag_inverse, row_size):
    local_rows, local_cols = ancestor_inverse.shape
    snodes, tile = diag_inverse.shape[:2]
    held = l_rows.shape[1] // tile
    cfg = sizes(row_size, snodes, tile, held, local_rows, local_cols)
    phases, blocks, shares, depth = cfg["phases"], cfg["blocks"], cfg["shares"], cfg["depth"]
    strip = tile // PARTS // 2
    groups = phases // 2
    total = inverse.shape[1]
    half = shares * tile
    kind = ancestor_inverse.dtype
    dma = pltpu.SemaphoreType.DMA
    scratch = [pltpu.VMEM((total, strip, LANES), kind) for _ in range(phases)]
    scratch += [pltpu.VMEM((PARTS, blocks, strip, LANES), kind) for _ in range(phases)]
    scratch += [
        pltpu.VMEM((half, local_cols), kind),
        pltpu.VMEM((2, tile, local_cols), kind),
        pltpu.VMEM(l_rows.shape, kind),
        pltpu.VMEM(diag_inverse.shape, kind),
        pltpu.VMEM((phases, PARTS, held, strip, LANES), kind),
        pltpu.VMEM((phases, blocks, strip, LANES), kind),
        pltpu.VMEM((groups, shares, LANES, tile), kind),
        pltpu.VMEM((groups, shares, LANES, tile), kind),
        pltpu.VMEM((snodes, tile, half), kind),
        pltpu.VMEM((half, LANES), jnp.float32),
        dma((phases, 3)),
        dma((phases, 3)),
        dma((phases, 5)),
        dma((phases, depth)),
        dma((phases,)),
        dma((phases,)),
        dma((phases, 2, 2)),
        dma((phases, 2, 2)),
        dma((phases, 2)),
        dma((phases, 2)),
        dma((groups, shares)),
        dma((groups, shares)),
        dma((shares,)),
        dma((2,)),
        dma((snodes, 2)),
        dma((snodes,)),
    ]
    smem = pl.BlockSpec(memory_space=pltpu.SMEM)
    anywhere = pl.BlockSpec(memory_space=pl.ANY)
    return pl.pallas_call(
        functools.partial(fused_kernel, cfg),
        out_shape=jax.ShapeDtypeStruct((snodes, tile, half), kind),
        in_specs=[smem, smem, anywhere, anywhere, anywhere],
        out_specs=anywhere,
        scratch_shapes=scratch,
        compiler_params=pltpu.CompilerParams(
            collective_id=0, has_side_effects=True, vmem_limit_bytes=67043328
        ),
        name="fused",
    )(inverse, mask, ancestor_inverse, l_rows, diag_inverse)


def fast(ancestor_inverse, fill_mask, block_order, l_rows, diag_inverse):
    packed = jnp.arange(block_order.shape[1], dtype=jnp.int32)
    inverse = jnp.sum(
        jnp.where(block_order[:, None, :] == packed[None, :, None], packed[None, None, :], 0), axis=2
    ).astype(jnp.int32)
    return fused(
        inverse, fill_mask, ancestor_inverse, l_rows, diag_inverse, lax.axis_size("row")
    )


def plain(ancestor_inverse, fill_mask, block_order, l_rows, diag_inverse):
    row_index = lax.axis_index("row")
    col_index = lax.axis_index("col")
    local_rows, local_cols = ancestor_inverse.shape
    snode_count, tile_size = diag_inverse.shape[:2]
    block_count = fill_mask.shape[0]
    row_blocks = local_rows // tile_size
    col_blocks = local_cols // tile_size
    normed = jnp.einsum(
        "sxy,syz->sxz", l_rows, diag_inverse, preferred_element_type=jnp.float32
    ).astype(jnp.bfloat16)
    wanted = col_index * col_blocks + jnp.arange(col_blocks, dtype=jnp.int32)
    everything = lax.all_gather(normed, ("row", "col"), axis=1, tiled=True)
    pieces = everything.reshape(snode_count, block_count, tile_size, tile_size)
    selector = (block_order[:, None, :] == wanted[None, :, None]).astype(jnp.bfloat16)
    columns = jnp.einsum(
        "saq,sqxy->saxy", selector, pieces, preferred_element_type=jnp.float32
    ).astype(jnp.bfloat16)
    stacked = columns.transpose(1, 2, 0, 3).reshape(local_cols, snode_count * tile_size)
    tile_gate = lax.dynamic_slice(
        fill_mask, (row_index * row_blocks, col_index * col_blocks), (row_blocks, col_blocks)
    ).astype(jnp.bfloat16)
    masked = (
        ancestor_inverse.reshape(row_blocks, tile_size, col_blocks, tile_size)
        * tile_gate[:, None, :, None]
    ).reshape(local_rows, local_cols)
    share_rows = local_rows // lax.axis_size("col")
    own_rows = lax.psum_scatter(
        (-jnp.dot(masked, stacked, preferred_element_type=jnp.float32)).astype(jnp.bfloat16),
        "col",
        scatter_dimension=0,
        tiled=True,
    ).astype(jnp.float32)
    return (
        own_rows.reshape(share_rows, snode_count, tile_size).transpose(1, 2, 0).astype(jnp.bfloat16)
    )


def per_device(ancestor_inverse, fill_mask, block_order, l_rows, diag_inverse):
    tile = diag_inverse.shape[1]
    col_size = lax.axis_size("col")
    if (
        col_size == 2
        and lax.axis_size("row") in (4, 8)
        and tile == 2 * LANES
        and diag_inverse.shape[0] == 2
        and l_rows.shape[1] % tile == 0
        and ancestor_inverse.shape[0] % (col_size * tile) == 0
    ):
        return fast(ancestor_inverse, fill_mask, block_order, l_rows, diag_inverse)
    return plain(ancestor_inverse, fill_mask, block_order, l_rows, diag_inverse)


def solution(mesh):
    return jax.shard_map(
        per_device,
        mesh=mesh,
        in_specs=(
            P(("snode", "row"), "col"),
            P("snode", None),
            P("snode", None),
            P("snode", ("row", "col"), None),
            P("snode", None, None),
        ),
        out_specs=P("snode", None, ("row", "col")),
        check_vma=False,
    )
```

```python
import functools

import jax
import jax.numpy as jnp
from jax import lax
from jax.experimental import pallas as pl
from jax.experimental.pallas import tpu as pltpu
from jax.sharding import PartitionSpec as P

MESH = pl.DeviceIdType.MESH
LANES = 128
PARTS = 4
AWAY = (0, 0, 0, 0, 14, 16, 18, 10)


def sizes(row_size, snodes, tile, held, local_rows, local_cols):
    blocks = local_cols // tile
    return dict(
        depth=row_size // 2,
        halves=tile // LANES,
        phases=2 * snodes * (tile // LANES),
        snodes=snodes,
        tile=tile,
        held=held,
        blocks=blocks,
        shares=local_rows // (2 * tile),
        away=[blocks * n // 40 for n in AWAY],
    )


def fused_kernel(cfg, order_hbm, mask_hbm, a_ref, l_ref, d_ref, out_ref, *rest):
    depth, halves, phases = cfg["depth"], cfg["halves"], cfg["phases"]
    snodes, tile, held = cfg["snodes"], cfg["tile"], cfg["held"]
    blocks, shares, away = cfg["blocks"], cfg["shares"], cfg["away"]
    lanes, rest = rest[:phases], rest[phases:]
    cols, rest = rest[:phases], rest[phases:]
    (
        theirs_ref,
        mine_ref,
        l_vm,
        d_vm,
        order_vm,
        table_vm,
        inv_ref,
        mask_ref,
        own_ref,
        pick_ref,
        give_ref,
        take_ref,
        res_ref,
        part_ref,
        b_send,
        c_send,
        y_send,
        x_send,
        o_send,
        b_recv,
        c_recv,
        y_recv,
        x_recv,
        f_recv,
        o_recv,
        a_sem,
        m_sem,
        in_sem,
        out_sem,
    ) = rest
    strip = tile // PARTS // 2
    plane = PARTS * held

    row = lax.axis_index("row")
    y = lax.axis_index("col")
    core = lax.axis_index("snode")
    z = row // 2
    x = row % 2
    me = x * 2 + y
    lane_x = (1 - x) * 2 + y
    lane_y = x * 2 + 1 - y
    lane_d = (1 - x) * 2 + 1 - y
    slot = (row * 2 + y) * held

    def at(zz, xx, yy):
        return (zz * 2 + xx, yy, core)

    sides = [(at(z, 1 - x, y), lane_x), (at(z, x, 1 - y), lane_y), (at(z, 1 - x, 1 - y), lane_d)]
    to_x, to_y = sides[0][0], sides[1][0]
    pair = at(z + 1 - 2 * (z % 2), x, y)
    reach = [dz for dz in (2, -2, 1, -1) if abs(dz) < depth]

    def exists(dz):
        return z + dz < depth if dz > 0 else z + dz >= 0

    inner = jnp.logical_and(z >= 1, z + 1 < depth)
    low = z * 2 < depth
    far = jnp.where(low, z + 2, z - 2)
    near = jnp.where(low, z - 1, z + 1)

    loads = []
    for s in range(snodes):
        loads.append(pltpu.make_async_copy(l_ref.at[s], l_vm.at[s], in_sem.at[s, 0]))
        loads.append(pltpu.make_async_copy(d_ref.at[s], d_vm.at[s], in_sem.at[s, 1]))
    order_load = pltpu.make_async_copy(order_hbm, order_vm, in_sem.at[snodes, 0])
    mask_load = pltpu.make_async_copy(mask_hbm, mask_ref, in_sem.at[snodes, 1])
    table_move = pltpu.make_async_copy(table_vm, inv_ref, in_sem.at[snodes, 0])
    for c in loads[:2] + [order_load] + loads[2:]:
        c.start()

    def theirs_load(i):
        return pltpu.make_async_copy(
            a_ref.at[pl.ds(((1 - y) * shares + i) * tile, tile)],
            theirs_ref.at[pl.ds(i * tile, tile)],
            a_sem.at[i],
        )

    def mine_load(g):
        return pltpu.make_async_copy(
            a_ref.at[pl.ds((y * shares + g % shares) * tile, tile)],
            mine_ref.at[g % 2],
            m_sem.at[g % 2],
        )

    barrier = pltpu.get_barrier_semaphore()
    for dev, _ in sides:
        pl.semaphore_signal(barrier, inc=1, device_id=dev, device_id_type=MESH)
    for dz in reach:

        @pl.when(exists(dz))
        def _():
            pl.semaphore_signal(barrier, inc=1, device_id=at(z + dz, x, y), device_id_type=MESH)

    def normalize(g):
        s, h = g // halves, g % halves
        rows = jnp.dot(
            l_vm[s], d_vm[s, :, h * LANES : (h + 1) * LANES], preferred_element_type=jnp.float32
        ).reshape(held, PARTS, 2, strip, LANES)
        for u in range(2):
            own_ref[2 * g + u] = rows[:, :, u].astype(own_ref.dtype).transpose(1, 0, 2, 3)
            lanes[2 * g + u][pl.ds(slot, held)] = own_ref[2 * g + u, me]

    for c in loads[:2]:
        c.wait()
    normalize(0)

    @pl.when(inner)
    def _():
        pl.semaphore_wait(barrier, len(sides) + 3)

    @pl.when(jnp.logical_not(inner))
    def _():
        pl.semaphore_wait(barrier, len(sides) + min(2, depth - 1))

    def remote(src, dst, send, recv, dev):
        return pltpu.make_async_remote_copy(
            src_ref=src, dst_ref=dst, send_sem=send, recv_sem=recv, device_id=dev, device_id_type=MESH
        )

    def guarded(cond, fn):
        if cond is None:
            fn()
        else:
            pl.when(cond)(fn)

    def start(make, cond=None):
        guarded(cond, lambda: make().start())

    def arrive(like, sem):
        pltpu.make_async_copy(like, like, sem).wait()

    def b_copy(p, k):
        dev, lane = sides[k]
        return remote(
            own_ref.at[p, lane], lanes[p].at[pl.ds(slot, held)], b_send, b_recv.at[p], dev
        )

    def spread(p):
        for k in (2, 0, 1):
            start(lambda k=k: b_copy(p, k))

    def far_of(zz):
        return jnp.where(zz * 2 < depth, zz + 2, zz - 2)

    def c_copy(p, source, target, index):
        span = pl.ds(source * plane, plane)
        kind = jnp.where(far_of(target) == source, 1, 0)
        return remote(
            lanes[p].at[span],
            lanes[p].at[span],
            c_send.at[index],
            c_recv.at[p, kind],
            at(target, x, y),
        )

    def climb(p):
        arrive(own_ref.at[p, 0:3], b_recv.at[p])
        for n, dz in enumerate(reach):
            start(lambda n=n, dz=dz: c_copy(p, z, z + dz, n), exists(dz))

    def far_arrives(p):
        arrive(lanes[p].at[0:plane], c_recv.at[p, 1])

    def relay(p):
        if depth < 4:
            return
        guarded(inner if p == phases - 1 else None, lambda: far_arrives(p))
        start(lambda: c_copy(p, far, near, len(reach)), inner)

    def climbed(p):
        others = depth - 1
        if depth >= 4:
            others -= 1
            if p == phases - 1:
                guarded(jnp.logical_not(inner), lambda: far_arrives(p))
        arrive(lanes[p].at[0 : others * plane], c_recv.at[p, 0])

    def y_copy(p):
        return remote(pick_ref.at[p], cols[p].at[me], y_send, y_recv.at[p], to_y)

    def pieces(p):
        first, rest = away[p], blocks - 2 * away[p]
        if not first:
            return [(0, 0, blocks)]
        return [(0, blocks - first, first)] + ([(first, first, rest)] if rest else [])

    def x_slot(p, kind):
        before = sum(3 if away[n] else 1 for n in range(p))
        return before + (kind if away[p] else 0)

    def x_copy(p, k, n):
        lane = (me, lane_y)[k]
        even, odd, size = pieces(p)[n]
        span = pl.ds(even + (z % 2) * (odd - even), size)
        sem = x_recv.at[x_slot(p, k if away[p] and n == 0 else 2)]
        return remote(cols[p].at[lane, span], cols[p].at[lane, span], x_send.at[k], sem, to_x)

    def cross(p, k):
        for n in range(len(pieces(p))):
            start(lambda n=n: x_copy(p, k, n))

    def f_copy(p, k):
        lane = (lane_x, lane_d)[k]
        span = pl.ds((z % 2) * (blocks - away[p]), away[p])
        sem = f_recv.at[sum(1 for n in range(p) if away[n])]
        return remote(cols[p].at[lane, span], cols[p].at[lane, span], x_send.at[k], sem, pair)

    def sort(p):
        climbed(p)
        if p == 0:
            table_move.wait()
        s = p // (2 * halves)

        def pick(j, carry):
            pick_ref[p, j] = lanes[p][inv_ref[s, (1 - y) * blocks + j, 0]]
            cols[p][me, j] = lanes[p][inv_ref[s, y * blocks + j, 0]]
            return carry

        lax.fori_loop(0, blocks, pick, 0)
        start(lambda: y_copy(p))
        cross(p, 0)

    def pass_on(p):
        y_copy(p).wait_recv()
        cross(p, 1)

    def forward(p, k):
        if away[p]:
            arrive(cols[p].at[0, 0 : away[p]], x_recv.at[x_slot(p, k)])
            start(lambda: f_copy(p, k))

    def crossed(p):
        size = blocks - 2 * away[p]
        if size:
            arrive(cols[p].at[0:2, 0:size], x_recv.at[x_slot(p, 2)])

    def forwarded(p):
        if away[p]:
            arrive(cols[p].at[0:2, 0 : away[p]], f_copy_sem(p))

    def f_copy_sem(p):
        return f_recv.at[sum(1 for n in range(p) if away[n])]

    def make_table():
        order_load.wait()
        shape = (inv_ref.shape[1], order_hbm.shape[1])
        wanted = lax.broadcasted_iota(jnp.int32, shape, 0)
        packed = lax.broadcasted_iota(jnp.int32, shape, 1)
        for s in range(snodes):
            found = jnp.where(order_vm[s : s + 1, :] == wanted, packed, 0)
            place = jnp.max(found, axis=1, keepdims=True)
            table_vm[s] = jnp.broadcast_to(place, table_vm.shape[1:])
        table_move.start()

    def gate_of(i, j):
        return mask_ref[i, y * blocks + j].astype(jnp.float32).astype(theirs_ref.dtype)

    def gate_theirs():
        first = row * 2 * shares + (1 - y) * shares

        def one_row(i, carry):
            pltpu.make_async_copy(
                a_ref.at[pl.ds(0, tile)], theirs_ref.at[pl.ds(i * tile, tile)], a_sem.at[i]
            ).wait()
            rows = pl.ds(pl.multiple_of(i * tile, tile), tile)

            def one(j, carry):
                span = pl.ds(pl.multiple_of(j * tile, tile), tile)
                theirs_ref[rows, span] = theirs_ref[rows, span] * gate_of(first + i, j)
                return carry

            return lax.fori_loop(0, blocks, one, carry)

        lax.fori_loop(0, shares, one_row, 0)

    step = max(n for n in range(1, 5) if blocks % n == 0)
    wide = max(n for n in range(1, 9) if blocks % n == 0)

    def stacked(strips):
        return jnp.stack(strips, axis=2).transpose(1, 0, 2, 3, 4).reshape(-1, LANES)

    def columns(g, c):
        js = slice(c * step, (c + 1) * step)
        return stacked([cols[2 * g + u][:, js] for u in range(2)])

    def o_copy(g, i):
        return remote(
            give_ref.at[g, i], take_ref.at[g, i], o_send, o_recv.at[g // halves, i], to_y
        )

    def send_block(g, i, total):
        give_ref[g, i] = (-total).T.astype(give_ref.dtype)
        o_copy(g, i).start()

    def theirs(g, lo, hi):
        def block(i, carry):
            rows = pl.ds(pl.multiple_of(i * tile, tile), tile)
            total = jnp.zeros((tile, LANES), jnp.float32)
            for c in range(blocks // step):
                total += jnp.dot(
                    theirs_ref[rows, c * step * tile : (c + 1) * step * tile],
                    columns(g, c),
                    preferred_element_type=jnp.float32,
                )
            send_block(g, i, total)
            return carry

        lax.fori_loop(lo, hi, block, 0)

    def side_dot(groups, side, rows):
        total = jnp.zeros((tile, len(groups) * LANES), jnp.float32)
        for c in range(blocks // wide):
            left = jnp.concatenate(
                [
                    theirs_ref[rows, pl.ds(pl.multiple_of(j * tile + side * LANES, LANES), LANES)]
                    for j in range(c * wide, (c + 1) * wide)
                ],
                axis=1,
            )
            right = [
                stacked(
                    [cols[2 * g + u][pl.ds(side * 2, 2), c * wide : (c + 1) * wide] for u in range(2)]
                )
                for g in groups
            ]
            total += jnp.dot(
                left, jnp.concatenate(right, axis=1), preferred_element_type=jnp.float32
            )
        return total

    def theirs_near(groups):
        def block(i, carry):
            rows = pl.ds(pl.multiple_of(i * tile, tile), tile)
            part_ref[rows, : len(groups) * LANES] = side_dot(groups, x, rows)
            return carry

        lax.fori_loop(0, shares, block, 0)

    def theirs_far(g, n):
        def block(i, carry):
            rows = pl.ds(pl.multiple_of(i * tile, tile), tile)
            total = side_dot([g], 1 - x, rows)
            send_block(g, i, total + part_ref[rows, n * LANES : (n + 1) * LANES])
            if g == phases // 2 - 1:

                @pl.when(i + 2 < shares)
                def _():
                    late_load(i).start()

            return carry

        lax.fori_loop(0, shares, block, 0)

    def late_load(i):
        return pltpu.make_async_copy(
            a_ref.at[pl.ds((y * shares + 2 + i) * tile, tile)],
            theirs_ref.at[pl.ds(i * tile, tile)],
            a_sem.at[i],
        )

    def mine(s, lo, hi, late=False):
        first = row * 2 * shares + y * shares

        def block(i, carry):
            n = s * shares + i
            if late:
                late_load(i - 2).wait()
                source = theirs_ref.at[pl.ds(pl.multiple_of((i - 2) * tile, tile), tile)]
            else:
                mine_load(n).wait()
                source = mine_ref.at[n % 2]
            total = jnp.zeros((tile, tile), jnp.float32)
            for c in range(blocks // step):
                left = jnp.concatenate(
                    [
                        source[:, j * tile : (j + 1) * tile] * gate_of(first + i, j)
                        for j in range(c * step, (c + 1) * step)
                    ],
                    axis=1,
                )
                right = jnp.concatenate(
                    [columns(s * halves + h, c) for h in range(halves)], axis=1
                )
                total += jnp.dot(left, right, preferred_element_type=jnp.float32)

            if s == 0:
                mine_load(n + 2).start()

            total = (-total).T
            rows = pl.ds(pl.multiple_of(i * tile, tile), tile)
            both = pl.ds(s * halves, halves)
            arrive(take_ref.at[both, i], o_recv.at[s, i])
            for h in range(halves):
                span = slice(h * LANES, (h + 1) * LANES)
                res_ref[s, span, rows] = (
                    total[span] + take_ref[s * halves + h, i].astype(jnp.float32)
                ).astype(res_ref.dtype)
            pltpu.make_async_copy(
                res_ref.at[s, :, rows], out_ref.at[s, :, rows], out_sem.at[s]
            ).start()
            return carry

        lax.fori_loop(lo, hi, block, 0)

    spread(0)
    spread(1)
    mask_load.start()
    for i in range(shares):
        theirs_load(i).start()
    for n in range(2):
        mine_load(n).start()
    for c in loads[2:]:
        c.wait()
    for g in range(1, phases // 2):
        normalize(g)
        spread(2 * g)
        spread(2 * g + 1)
    climb(0)
    make_table()
    mask_load.wait()
    gate_theirs()
    relay(0)
    climb(1)
    sort(0)
    relay(1)
    climb(2)
    pass_on(0)
    sort(1)
    relay(2)
    climb(3)
    pass_on(1)
    sort(2)
    relay(3)
    climb(4)
    crossed(0)
    crossed(1)
    pass_on(2)
    sort(3)
    theirs(0, 0, 3)
    relay(4)
    climb(5)
    theirs(0, 3, 5)
    pass_on(3)
    sort(4)
    relay(5)
    climb(6)
    crossed(2)
    theirs_near([1])
    pass_on(4)
    sort(5)
    relay(6)
    climb(7)
    crossed(3)
    theirs_far(1, 0)
    pass_on(5)
    sort(6)
    relay(7)
    forward(4, 0)
    forward(4, 1)
    mine(0, 0, 3)
    pass_on(6)
    sort(7)
    forward(5, 0)
    forward(5, 1)
    mine(0, 3, 5)
    forward(6, 0)
    crossed(4)
    crossed(5)
    pass_on(7)
    forward(6, 1)
    theirs_near([2, 3])
    forward(7, 0)
    forward(7, 1)
    forwarded(4)
    forwarded(5)
    theirs_far(2, 0)
    crossed(6)
    crossed(7)
    forwarded(6)
    forwarded(7)
    theirs_far(3, 1)
    mine(1, 0, 2)
    mine(1, 2, 5, True)
    for s in range(snodes):
        pltpu.make_async_copy(res_ref.at[s], out_ref.at[s], out_sem.at[s]).wait()
    arrive(own_ref.at[:, 0:3], b_send)
    for n, dz in enumerate(reach):
        guarded(exists(dz), lambda n=n: arrive(own_ref, c_send.at[n]))
    if depth >= 4:
        guarded(inner, lambda: arrive(own_ref, c_send.at[len(reach)]))
    arrive(pick_ref, y_send)
    for k in range(2):
        arrive(pick_ref, x_send.at[k])
    arrive(give_ref, o_send)


def fused(order, mask, ancestor_inverse, l_rows, diag_inverse, row_size):
    local_rows, local_cols = ancestor_inverse.shape
    snodes, tile = diag_inverse.shape[:2]
    held = l_rows.shape[1] // tile
    cfg = sizes(row_size, snodes, tile, held, local_rows, local_cols)
    phases, blocks, shares, depth = cfg["phases"], cfg["blocks"], cfg["shares"], cfg["depth"]
    strip = tile // PARTS // 2
    groups = phases // 2
    halves = cfg["halves"]
    away = cfg["away"]
    total = order.shape[1]
    half = shares * tile
    kind = ancestor_inverse.dtype
    dma = pltpu.SemaphoreType.DMA
    scratch = [pltpu.VMEM((total, strip, LANES), kind) for _ in range(phases)]
    scratch += [pltpu.VMEM((PARTS, blocks, strip, LANES), kind) for _ in range(phases)]
    scratch += [
        pltpu.VMEM((half, local_cols), kind),
        pltpu.VMEM((2, tile, local_cols), kind),
        pltpu.VMEM(l_rows.shape, kind),
        pltpu.VMEM(diag_inverse.shape, kind),
        pltpu.VMEM(order.shape, jnp.int32),
        pltpu.VMEM((snodes, total, LANES), jnp.int32),
        pltpu.SMEM((snodes, total, LANES), jnp.int32),
        pltpu.SMEM(mask.shape, jnp.int32),
        pltpu.VMEM((phases, PARTS, held, strip, LANES), kind),
        pltpu.VMEM((phases, blocks, strip, LANES), kind),
        pltpu.VMEM((groups, shares, LANES, tile), kind),
        pltpu.VMEM((groups, shares, LANES, tile), kind),
        pltpu.VMEM((snodes, tile, half), kind),
        pltpu.VMEM((half, halves * LANES), jnp.float32),
        dma,
        dma((5,)),
        dma,
        dma((2,)),
        dma,
        dma((phases,)),
        dma((phases, 2)),
        dma((phases,)),
        dma((sum(3 if n else 1 for n in away),)),
        dma((max(1, sum(1 for n in away if n)),)),
        dma((snodes, shares)),
        dma((shares,)),
        dma((2,)),
        dma((snodes + 1, 2)),
        dma((snodes,)),
    ]
    anywhere = pl.BlockSpec(memory_space=pl.ANY)
    return pl.pallas_call(
        functools.partial(fused_kernel, cfg),
        out_shape=jax.ShapeDtypeStruct((snodes, tile, half), kind),
        in_specs=[anywhere] * 5,
        out_specs=anywhere,
        scratch_shapes=scratch,
        compiler_params=pltpu.CompilerParams(
            collective_id=0, has_side_effects=True, vmem_limit_bytes=67043328
        ),
        name="fused",
    )(order, mask, ancestor_inverse, l_rows, diag_inverse)


def fast(ancestor_inverse, fill_mask, block_order, l_rows, diag_inverse):
    return fused(
        block_order, fill_mask, ancestor_inverse, l_rows, diag_inverse, lax.axis_size("row")
    )


def plain(ancestor_inverse, fill_mask, block_order, l_rows, diag_inverse):
    row_index = lax.axis_index("row")
    col_index = lax.axis_index("col")
    local_rows, local_cols = ancestor_inverse.shape
    snode_count, tile_size = diag_inverse.shape[:2]
    block_count = fill_mask.shape[0]
    row_blocks = local_rows // tile_size
    col_blocks = local_cols // tile_size
    normed = jnp.einsum(
        "sxy,syz->sxz", l_rows, diag_inverse, preferred_element_type=jnp.float32
    ).astype(jnp.bfloat16)
    wanted = col_index * col_blocks + jnp.arange(col_blocks, dtype=jnp.int32)
    everything = lax.all_gather(normed, ("row", "col"), axis=1, tiled=True)
    pieces = everything.reshape(snode_count, block_count, tile_size, tile_size)
    selector = (block_order[:, None, :] == wanted[None, :, None]).astype(jnp.bfloat16)
    columns = jnp.einsum(
        "saq,sqxy->saxy", selector, pieces, preferred_element_type=jnp.float32
    ).astype(jnp.bfloat16)
    stacked = columns.transpose(1, 2, 0, 3).reshape(local_cols, snode_count * tile_size)
    tile_gate = lax.dynamic_slice(
        fill_mask, (row_index * row_blocks, col_index * col_blocks), (row_blocks, col_blocks)
    ).astype(jnp.bfloat16)
    masked = (
        ancestor_inverse.reshape(row_blocks, tile_size, col_blocks, tile_size)
        * tile_gate[:, None, :, None]
    ).reshape(local_rows, local_cols)
    share_rows = local_rows // lax.axis_size("col")
    own_rows = lax.psum_scatter(
        (-jnp.dot(masked, stacked, preferred_element_type=jnp.float32)).astype(jnp.bfloat16),
        "col",
        scatter_dimension=0,
        tiled=True,
    ).astype(jnp.float32)
    return (
        own_rows.reshape(share_rows, snode_count, tile_size).transpose(1, 2, 0).astype(jnp.bfloat16)
    )


def per_device(ancestor_inverse, fill_mask, block_order, l_rows, diag_inverse):
    tile = diag_inverse.shape[1]
    col_size = lax.axis_size("col")
    if (
        col_size == 2
        and lax.axis_size("row") in (4, 8)
        and tile == 2 * LANES
        and diag_inverse.shape[0] == 2
        and l_rows.shape[1] % tile == 0
        and ancestor_inverse.shape[0] % (col_size * tile) == 0
    ):
        return fast(ancestor_inverse, fill_mask, block_order, l_rows, diag_inverse)
    return plain(ancestor_inverse, fill_mask, block_order, l_rows, diag_inverse)


def solution(mesh):
    return jax.shard_map(
        per_device,
        mesh=mesh,
        in_specs=(
            P(("snode", "row"), "col"),
            P("snode", None),
            P("snode", None),
            P("snode", ("row", "col"), None),
            P("snode", None, None),
        ),
        out_specs=P("snode", None, ("row", "col")),
        check_vma=False,
    )
```

```python
import functools

import jax
import jax.numpy as jnp
from jax import lax
from jax.experimental import pallas as pl
from jax.experimental.pallas import tpu as pltpu
from jax.sharding import PartitionSpec as P

MESH = pl.DeviceIdType.MESH
LANES = 128
PARTS = 4
AWAY = (0, 0, 0, 0, 16, 18, 20, 0)
PICKS = 2


def sizes(row_size, snodes, tile, held, local_rows, local_cols):
    blocks = local_cols // tile
    return dict(
        depth=row_size // 2,
        halves=tile // LANES,
        spans=[(b, 0, tile // PARTS // 2) for b in range(2 * snodes * (tile // LANES))],
        snodes=snodes,
        tile=tile,
        held=held,
        blocks=blocks,
        shares=local_rows // (2 * tile),
        away=[blocks * n // 40 for n in AWAY],
    )


def fused_kernel(cfg, order_hbm, mask_hbm, a_ref, l_ref, d_ref, out_ref, *rest):
    depth, halves, spans = cfg["depth"], cfg["halves"], cfg["spans"]
    phases, buffers = len(spans), spans[-1][0] + 1
    snodes, tile, held = cfg["snodes"], cfg["tile"], cfg["held"]
    blocks, shares, away = cfg["blocks"], cfg["shares"], cfg["away"]
    lanes, rest = rest[:phases], rest[phases:]
    cols, rest = rest[:buffers], rest[buffers:]
    (
        theirs_ref,
        mine_ref,
        d_vm,
        order_vm,
        table_vm,
        inv_ref,
        mask_ref,
        own_ref,
        pick_ref,
        give_ref,
        take_ref,
        res_ref,
        part_ref,
        mine_part_ref,
        b_send,
        c_send,
        y_send,
        x_send,
        o_send,
        b_recv,
        c_recv,
        y_recv,
        x_recv,
        f_recv,
        o_recv,
        a_sem,
        m_sem,
        in_sem,
        out_sem,
    ) = rest
    strip = tile // PARTS // 2
    plane = PARTS * held

    row = lax.axis_index("row")
    y = lax.axis_index("col")
    core = lax.axis_index("snode")
    z = row // 2
    x = row % 2
    me = x * 2 + y
    lane_x = (1 - x) * 2 + y
    lane_y = x * 2 + 1 - y
    lane_d = (1 - x) * 2 + 1 - y
    slot = (row * 2 + y) * held

    def at(zz, xx, yy):
        return (zz * 2 + xx, yy, core)

    sides = [(at(z, 1 - x, y), lane_x), (at(z, x, 1 - y), lane_y), (at(z, 1 - x, 1 - y), lane_d)]
    to_x, to_y = sides[0][0], sides[1][0]
    pair = at(z + 1 - 2 * (z % 2), x, y)
    reach = [dz for dz in (2, -2, 1, -1) if abs(dz) < depth]

    def exists(dz):
        return z + dz < depth if dz > 0 else z + dz >= 0

    inner = jnp.logical_and(z >= 1, z + 1 < depth)
    low = z * 2 < depth
    far = jnp.where(low, z + 2, z - 2)
    near = jnp.where(low, z - 1, z + 1)

    def packed(s):
        return theirs_ref.at[0 : held * tile, s * tile : (s + 1) * tile]

    loads = []
    for s in range(snodes):
        loads.append(pltpu.make_async_copy(l_ref.at[s], packed(s), in_sem.at[s, 0]))
        loads.append(pltpu.make_async_copy(d_ref.at[s], d_vm.at[s], in_sem.at[s, 1]))
    order_load = pltpu.make_async_copy(order_hbm, order_vm, in_sem.at[snodes, 0])
    mask_load = pltpu.make_async_copy(mask_hbm, mask_ref, in_sem.at[snodes, 1])
    table_move = pltpu.make_async_copy(table_vm, inv_ref, in_sem.at[snodes, 0])
    for c in loads[:2] + [order_load] + loads[2:]:
        c.start()

    def theirs_load(i):
        return pltpu.make_async_copy(
            a_ref.at[pl.ds(((1 - y) * shares + i) * tile, tile)],
            theirs_ref.at[pl.ds(i * tile, tile)],
            a_sem.at[i],
        )

    def mine_load(n):
        again = 2 * shares - 1
        i = jnp.where(n < shares, n, jnp.where(n < again, n - shares, n - again))
        return pltpu.make_async_copy(
            a_ref.at[pl.ds((y * shares + i) * tile, tile)], mine_ref.at[n % 2], m_sem.at[n % 2]
        )

    barrier = pltpu.get_barrier_semaphore()
    for dev, _ in sides:
        pl.semaphore_signal(barrier, inc=1, device_id=dev, device_id_type=MESH)
    for dz in reach:

        @pl.when(exists(dz))
        def _():
            pl.semaphore_signal(barrier, inc=1, device_id=at(z + dz, x, y), device_id_type=MESH)

    def normalize(g):
        s, h = g // halves, g % halves
        rows = jnp.dot(
            theirs_ref[0 : held * tile, s * tile : (s + 1) * tile],
            d_vm[s, :, h * LANES : (h + 1) * LANES], preferred_element_type=jnp.float32
        ).reshape(held, PARTS, 2, strip, LANES)
        for u in range(2):
            own_ref[2 * g + u] = rows[:, :, u].astype(own_ref.dtype).transpose(1, 0, 2, 3)
            for p, (b, at_row, size) in enumerate(spans):
                if b == 2 * g + u:
                    lanes[p][pl.ds(slot, held)] = own_ref[b, me, :, at_row : at_row + size]

    for c in loads[:2]:
        c.wait()
    normalize(0)

    @pl.when(inner)
    def _():
        pl.semaphore_wait(barrier, len(sides) + 3)

    @pl.when(jnp.logical_not(inner))
    def _():
        pl.semaphore_wait(barrier, len(sides) + min(2, depth - 1))

    def remote(src, dst, send, recv, dev):
        return pltpu.make_async_remote_copy(
            src_ref=src, dst_ref=dst, send_sem=send, recv_sem=recv, device_id=dev, device_id_type=MESH
        )

    def guarded(cond, fn):
        if cond is None:
            fn()
        else:
            pl.when(cond)(fn)

    def start(make, cond=None):
        guarded(cond, lambda: make().start())

    def arrive(like, sem):
        pltpu.make_async_copy(like, like, sem).wait()

    def part_of(p):
        b, at_row, size = spans[p]
        return b, slice(at_row, at_row + size)

    def strips(p, lane, span):
        b, part = part_of(p)
        return cols[b].at[lane, span, part]

    def picked(p):
        return pick_ref.at[p % PICKS]

    def b_copy(p, k):
        dev, lane = sides[k]
        b, part = part_of(p)
        return remote(
            own_ref.at[b, lane, :, part], lanes[p].at[pl.ds(slot, held)], b_send, b_recv.at[p], dev
        )

    def spread(p):
        for k in (2, 0, 1):
            start(lambda k=k: b_copy(p, k))

    def far_of(zz):
        return jnp.where(zz * 2 < depth, zz + 2, zz - 2)

    def c_copy(p, source, target, index):
        span = pl.ds(source * plane, plane)
        kind = jnp.where(far_of(target) == source, 1, 0)
        return remote(
            lanes[p].at[span],
            lanes[p].at[span],
            c_send.at[index],
            c_recv.at[p, kind],
            at(target, x, y),
        )

    def climb(p):
        b, part = part_of(p)
        arrive(own_ref.at[b, 0:3, :, part], b_recv.at[p])
        for n, dz in enumerate(reach):
            start(lambda n=n, dz=dz: c_copy(p, z, z + dz, n), exists(dz))

    def far_arrives(p):
        arrive(lanes[p].at[0:plane], c_recv.at[p, 1])

    def relay(p):
        if depth < 4:
            return
        guarded(inner if p == phases - 1 else None, lambda: far_arrives(p))
        start(lambda: c_copy(p, far, near, len(reach)), inner)

    def climbed(p):
        others = depth - 1
        if depth >= 4:
            others -= 1
            if p == phases - 1:
                guarded(jnp.logical_not(inner), lambda: far_arrives(p))
        arrive(lanes[p].at[0 : others * plane], c_recv.at[p, 0])

    def y_copy(p):
        return remote(
            picked(p), strips(p, me, slice(0, blocks)), y_send.at[p % PICKS], y_recv.at[p], to_y
        )

    def pieces(p):
        first, rest = away[p], blocks - 2 * away[p]
        if not first:
            return [(0, 0, blocks)]
        return [(0, blocks - first, first)] + ([(first, first, rest)] if rest else [])

    def x_slot(p, kind):
        before = sum(3 if away[n] else 1 for n in range(p))
        return before + (kind if away[p] else 0)

    def x_copy(p, k, n):
        lane = (me, lane_y)[k]
        even, odd, size = pieces(p)[n]
        span = pl.ds(even + (z % 2) * (odd - even), size)
        sem = x_recv.at[x_slot(p, k if away[p] and n == 0 else 2)]
        return remote(strips(p, lane, span), strips(p, lane, span), x_send.at[k], sem, to_x)

    def cross(p, k):
        for n in range(len(pieces(p))):
            start(lambda n=n: x_copy(p, k, n))

    def f_copy(p, k):
        lane = (lane_x, lane_d)[k]
        span = pl.ds((z % 2) * (blocks - away[p]), away[p])
        sem = f_recv.at[sum(1 for n in range(p) if away[n])]
        return remote(strips(p, lane, span), strips(p, lane, span), x_send.at[k], sem, pair)

    def sort(p):
        climbed(p)
        if p == 0:
            table_move.wait()
        b, part = part_of(p)
        s = b // (2 * halves)

        if p >= PICKS:
            arrive(picked(p), y_send.at[p % PICKS])

        def pick(j, carry):
            pick_ref[p % PICKS, j] = lanes[p][inv_ref[s, (1 - y) * blocks + j, 0]]
            cols[b][me, j, part] = lanes[p][inv_ref[s, y * blocks + j, 0]]
            return carry

        lax.fori_loop(0, blocks, pick, 0)
        start(lambda: y_copy(p))
        cross(p, 0)

    def pass_on(p):
        y_copy(p).wait_recv()
        cross(p, 1)

    def forward(p, k):
        if away[p]:
            arrive(strips(p, 0, slice(0, away[p])), x_recv.at[x_slot(p, k)])
            start(lambda: f_copy(p, k))

    def crossed(p):
        size = blocks - 2 * away[p]
        if size:
            arrive(strips(p, slice(0, 2), slice(0, size)), x_recv.at[x_slot(p, 2)])

    def forwarded(p):
        if away[p]:
            arrive(strips(p, slice(0, 2), slice(0, away[p])), f_copy_sem(p))

    def f_copy_sem(p):
        return f_recv.at[sum(1 for n in range(p) if away[n])]

    def make_table():
        order_load.wait()
        shape = (inv_ref.shape[1], order_hbm.shape[1])
        wanted = lax.broadcasted_iota(jnp.int32, shape, 0)
        packed = lax.broadcasted_iota(jnp.int32, shape, 1)
        for s in range(snodes):
            found = jnp.where(order_vm[s : s + 1, :] == wanted, packed, 0)
            place = jnp.max(found, axis=1, keepdims=True)
            table_vm[s] = jnp.broadcast_to(place, table_vm.shape[1:])
        table_move.start()

    def gate_of(i, j):
        return mask_ref[i, y * blocks + j].astype(jnp.float32).astype(theirs_ref.dtype)

    def gate(lo, hi):
        first = row * 2 * shares + (1 - y) * shares

        def one_row(i, carry):
            arrive(theirs_ref.at[pl.ds(i * tile, tile)], a_sem.at[i])
            rows = pl.ds(pl.multiple_of(i * tile, tile), tile)

            def one(j, carry):
                span = pl.ds(pl.multiple_of(j * tile, tile), tile)
                theirs_ref[rows, span] = theirs_ref[rows, span] * gate_of(first + i, j)
                return carry

            return lax.fori_loop(0, blocks, one, carry)

        lax.fori_loop(lo, hi, one_row, 0)

    step = max(n for n in range(1, 5) if blocks % n == 0)
    wide = max(n for n in range(1, 9) if blocks % n == 0)

    def stacked(strips):
        return jnp.stack(strips, axis=2).transpose(1, 0, 2, 3, 4).reshape(-1, LANES)

    def columns(g, c):
        js = slice(c * step, (c + 1) * step)
        return stacked([cols[2 * g + u][:, js] for u in range(2)])

    def o_copy(g, i):
        return remote(
            give_ref.at[g, i], take_ref.at[g, i], o_send, o_recv.at[g // halves, i], to_y
        )

    def send_block(g, i, total):
        give_ref[g, i] = (-total).T.astype(give_ref.dtype)
        o_copy(g, i).start()

    def theirs(g, lo, hi):
        def block(i, carry):
            rows = pl.ds(pl.multiple_of(i * tile, tile), tile)
            total = jnp.zeros((tile, LANES), jnp.float32)
            for c in range(blocks // step):
                total += jnp.dot(
                    theirs_ref[rows, c * step * tile : (c + 1) * step * tile],
                    columns(g, c),
                    preferred_element_type=jnp.float32,
                )
            send_block(g, i, total)
            return carry

        lax.fori_loop(lo, hi, block, 0)

    def side_dot(groups, side, left_of):
        total = jnp.zeros((tile, len(groups) * LANES), jnp.float32)
        for c in range(blocks // wide):
            left = jnp.concatenate(
                [
                    left_of(j, pl.ds(pl.multiple_of(j * tile + side * LANES, LANES), LANES))
                    for j in range(c * wide, (c + 1) * wide)
                ],
                axis=1,
            )
            right = [
                stacked(
                    [cols[2 * g + u][pl.ds(side * 2, 2), c * wide : (c + 1) * wide] for u in range(2)]
                )
                for g in groups
            ]
            total += jnp.dot(
                left, jnp.concatenate(right, axis=1), preferred_element_type=jnp.float32
            )
        return total

    def theirs_near(groups):
        def block(i, carry):
            rows = pl.ds(pl.multiple_of(i * tile, tile), tile)
            part_ref[rows, : len(groups) * LANES] = side_dot(groups, x, lambda j, span: theirs_ref[rows, span])
            return carry

        lax.fori_loop(0, shares, block, 0)

    def theirs_far(g, n):
        def block(i, carry):
            rows = pl.ds(pl.multiple_of(i * tile, tile), tile)
            total = side_dot([g], 1 - x, lambda j, span: theirs_ref[rows, span])
            send_block(g, i, total + part_ref[rows, n * LANES : (n + 1) * LANES])
            if g == buffers // 2 - 1:

                @pl.when(i + 2 < shares)
                def _():
                    late_load(i).start()

            return carry

        lax.fori_loop(0, shares, block, 0)

    def late_load(i):
        return pltpu.make_async_copy(
            a_ref.at[pl.ds((y * shares + 2 + i) * tile, tile)],
            theirs_ref.at[pl.ds(i * tile, tile)],
            a_sem.at[i],
        )

    def finish(s, i, total):
        total = (-total).T
        rows = pl.ds(pl.multiple_of(i * tile, tile), tile)
        both = pl.ds(s * halves, halves)
        arrive(take_ref.at[both, i], o_recv.at[s, i])
        for h in range(halves):
            span = slice(h * LANES, (h + 1) * LANES)
            res_ref[s, span, rows] = (
                total[span] + take_ref[s * halves + h, i].astype(jnp.float32)
            ).astype(res_ref.dtype)
        pltpu.make_async_copy(
            res_ref.at[s, :, rows], out_ref.at[s, :, rows], out_sem.at[s]
        ).start()

    first_mine = row * 2 * shares + y * shares

    def mine(s, lo, hi):
        def block(i, carry):
            n = i
            mine_load(n).wait()
            total = jnp.zeros((tile, tile), jnp.float32)
            for c in range(blocks // step):
                left = jnp.concatenate(
                    [
                        mine_ref[n % 2, :, j * tile : (j + 1) * tile] * gate_of(first_mine + i, j)
                        for j in range(c * step, (c + 1) * step)
                    ],
                    axis=1,
                )
                right = jnp.concatenate(
                    [columns(s * halves + h, c) for h in range(halves)], axis=1
                )
                total += jnp.dot(left, right, preferred_element_type=jnp.float32)
            mine_load(n + 2).start()
            finish(s, i, total)
            return carry

        lax.fori_loop(lo, hi, block, 0)

    tail = snodes - 1
    tail_groups = [tail * halves + h for h in range(halves)]

    def mine_near(lo, hi):
        def block(i, carry):
            n = shares + i
            mine_load(n).wait()
            rows = pl.ds(pl.multiple_of(i * tile, tile), tile)
            mine_part_ref[rows] = side_dot(
                tail_groups, x, lambda j, span: mine_ref[n % 2, :, span] * gate_of(first_mine + i, j)
            )
            mine_load(n + 2).start()
            return carry

        lax.fori_loop(lo, hi, block, 0)

    def mine_far(lo, hi, late, whole):
        def block(i, carry):
            n = 2 * shares - 1 + i
            if late:
                late_load(i - 2).wait()
                source = theirs_ref.at[pl.ds(pl.multiple_of((i - 2) * tile, tile), tile)]
            else:
                mine_load(n).wait()
                source = mine_ref.at[n % 2]
            rows = pl.ds(pl.multiple_of(i * tile, tile), tile)

            def gated(j, span):
                return source[:, span] * gate_of(first_mine + i, j)

            total = side_dot(tail_groups, 1 - x, gated)
            if whole:
                total += side_dot(tail_groups, x, gated)
            else:
                total += mine_part_ref[rows]
            finish(tail, i, total)
            return carry

        lax.fori_loop(lo, hi, block, 0)

    spread(0)
    mask_load.start()
    for n in range(2):
        mine_load(n).start()
    for c in loads[2:]:
        c.wait()
    for g in range(1, buffers // 2):
        normalize(g)
    for i in range(shares):
        theirs_load(i).start()
    climb(0)
    for p in range(1, phases):
        spread(p)
    make_table()
    relay(0)
    climb(1)
    mask_load.wait()
    gate(0, 2)
    sort(0)
    relay(1)
    climb(2)
    gate(2, 5)
    pass_on(0)
    sort(1)
    relay(2)
    climb(3)
    pass_on(1)
    sort(2)
    relay(3)
    climb(4)
    crossed(0)
    crossed(1)
    pass_on(2)
    sort(3)
    theirs(0, 0, 2)
    relay(4)
    climb(5)
    theirs(0, 2, 4)
    pass_on(3)
    theirs(0, 4, 5)
    sort(4)
    relay(5)
    climb(6)
    crossed(2)
    theirs_near([1])
    pass_on(4)
    sort(5)
    relay(6)
    climb(7)
    crossed(3)
    theirs_far(1, 0)
    pass_on(5)
    sort(6)
    relay(7)
    forward(4, 0)
    forward(4, 1)
    mine(0, 0, 3)
    pass_on(6)
    sort(7)
    forward(5, 0)
    forward(5, 1)
    mine(0, 3, 5)
    forward(6, 0)
    crossed(4)
    crossed(5)
    pass_on(7)
    theirs_near([2, 3])
    forward(6, 1)
    mine_near(0, 2)
    forward(7, 0)
    forwarded(4)
    forwarded(5)
    theirs_far(2, 0)
    forward(7, 1)
    mine_near(2, shares - 1)
    crossed(6)
    crossed(7)
    forwarded(6)
    forwarded(7)
    theirs_far(3, 1)
    mine_far(0, 2, False, False)
    mine_far(2, shares - 1, True, False)
    mine_far(shares - 1, shares, True, True)
    for s in range(snodes):
        pltpu.make_async_copy(res_ref.at[s], out_ref.at[s], out_sem.at[s]).wait()
    arrive(own_ref.at[:, 0:3], b_send)
    for n, dz in enumerate(reach):
        guarded(exists(dz), lambda n=n: arrive(own_ref, c_send.at[n]))
    if depth >= 4:
        guarded(inner, lambda: arrive(own_ref, c_send.at[len(reach)]))
    for k in range(PICKS):
        arrive(pick_ref.at[k], y_send.at[k])
    sent = buffers * strip * LANES // tile
    for k in range(2):
        arrive(theirs_ref.at[0:sent], x_send.at[k])
    arrive(give_ref, o_send)


def fused(order, mask, ancestor_inverse, l_rows, diag_inverse, row_size):
    local_rows, local_cols = ancestor_inverse.shape
    snodes, tile = diag_inverse.shape[:2]
    held = l_rows.shape[1] // tile
    cfg = sizes(row_size, snodes, tile, held, local_rows, local_cols)
    blocks, shares, depth = cfg["blocks"], cfg["shares"], cfg["depth"]
    phases, buffers = len(cfg["spans"]), cfg["spans"][-1][0] + 1
    strip = tile // PARTS // 2
    groups = buffers // 2
    halves = cfg["halves"]
    away = cfg["away"]
    total = order.shape[1]
    half = shares * tile
    kind = ancestor_inverse.dtype
    dma = pltpu.SemaphoreType.DMA
    scratch = [pltpu.VMEM((total, size, LANES), kind) for _, _, size in cfg["spans"]]
    scratch += [pltpu.VMEM((PARTS, blocks, strip, LANES), kind) for _ in range(buffers)]
    scratch += [
        pltpu.VMEM((half, local_cols), kind),
        pltpu.VMEM((2, tile, local_cols), kind),
        pltpu.VMEM(diag_inverse.shape, kind),
        pltpu.VMEM(order.shape, jnp.int32),
        pltpu.VMEM((snodes, total, LANES), jnp.int32),
        pltpu.SMEM((snodes, total, LANES), jnp.int32),
        pltpu.SMEM(mask.shape, jnp.int32),
        pltpu.VMEM((buffers, PARTS, held, strip, LANES), kind),
        pltpu.VMEM((PICKS, blocks, strip, LANES), kind),
        pltpu.VMEM((groups, shares, LANES, tile), kind),
        pltpu.VMEM((groups, shares, LANES, tile), kind),
        pltpu.VMEM((snodes, tile, half), kind),
        pltpu.VMEM((half, halves * LANES), jnp.float32),
        pltpu.VMEM((half, halves * LANES), jnp.float32),
        dma,
        dma((5,)),
        dma((PICKS,)),
        dma((2,)),
        dma,
        dma((phases,)),
        dma((phases, 2)),
        dma((phases,)),
        dma((sum(3 if n else 1 for n in away),)),
        dma((max(1, sum(1 for n in away if n)),)),
        dma((snodes, shares)),
        dma((shares,)),
        dma((2,)),
        dma((snodes + 1, 2)),
        dma((snodes,)),
    ]
    anywhere = pl.BlockSpec(memory_space=pl.ANY)
    return pl.pallas_call(
        functools.partial(fused_kernel, cfg),
        out_shape=jax.ShapeDtypeStruct((snodes, tile, half), kind),
        in_specs=[anywhere] * 5,
        out_specs=anywhere,
        scratch_shapes=scratch,
        compiler_params=pltpu.CompilerParams(
            collective_id=0, has_side_effects=True, vmem_limit_bytes=67043328
        ),
        name="fused",
    )(order, mask, ancestor_inverse, l_rows, diag_inverse)


def fast(ancestor_inverse, fill_mask, block_order, l_rows, diag_inverse):
    return fused(
        block_order, fill_mask, ancestor_inverse, l_rows, diag_inverse, lax.axis_size("row")
    )


def plain(ancestor_inverse, fill_mask, block_order, l_rows, diag_inverse):
    row_index = lax.axis_index("row")
    col_index = lax.axis_index("col")
    local_rows, local_cols = ancestor_inverse.shape
    snode_count, tile_size = diag_inverse.shape[:2]
    block_count = fill_mask.shape[0]
    row_blocks = local_rows // tile_size
    col_blocks = local_cols // tile_size
    normed = jnp.einsum(
        "sxy,syz->sxz", l_rows, diag_inverse, preferred_element_type=jnp.float32
    ).astype(jnp.bfloat16)
    wanted = col_index * col_blocks + jnp.arange(col_blocks, dtype=jnp.int32)
    everything = lax.all_gather(normed, ("row", "col"), axis=1, tiled=True)
    pieces = everything.reshape(snode_count, block_count, tile_size, tile_size)
    selector = (block_order[:, None, :] == wanted[None, :, None]).astype(jnp.bfloat16)
    columns = jnp.einsum(
        "saq,sqxy->saxy", selector, pieces, preferred_element_type=jnp.float32
    ).astype(jnp.bfloat16)
    stacked = columns.transpose(1, 2, 0, 3).reshape(local_cols, snode_count * tile_size)
    tile_gate = lax.dynamic_slice(
        fill_mask, (row_index * row_blocks, col_index * col_blocks), (row_blocks, col_blocks)
    ).astype(jnp.bfloat16)
    masked = (
        ancestor_inverse.reshape(row_blocks, tile_size, col_blocks, tile_size)
        * tile_gate[:, None, :, None]
    ).reshape(local_rows, local_cols)
    share_rows = local_rows // lax.axis_size("col")
    own_rows = lax.psum_scatter(
        (-jnp.dot(masked, stacked, preferred_element_type=jnp.float32)).astype(jnp.bfloat16),
        "col",
        scatter_dimension=0,
        tiled=True,
    ).astype(jnp.float32)
    return (
        own_rows.reshape(share_rows, snode_count, tile_size).transpose(1, 2, 0).astype(jnp.bfloat16)
    )


def per_device(ancestor_inverse, fill_mask, block_order, l_rows, diag_inverse):
    tile = diag_inverse.shape[1]
    col_size = lax.axis_size("col")
    if (
        col_size == 2
        and lax.axis_size("row") in (4, 8)
        and tile == 2 * LANES
        and diag_inverse.shape[0] == 2
        and l_rows.shape[1] * col_size <= ancestor_inverse.shape[0]
        and l_rows.shape[1] % tile == 0
        and ancestor_inverse.shape[0] % (col_size * tile) == 0
    ):
        return fast(ancestor_inverse, fill_mask, block_order, l_rows, diag_inverse)
    return plain(ancestor_inverse, fill_mask, block_order, l_rows, diag_inverse)


def solution(mesh):
    return jax.shard_map(
        per_device,
        mesh=mesh,
        in_specs=(
            P(("snode", "row"), "col"),
            P("snode", None),
            P("snode", None),
            P("snode", ("row", "col"), None),
            P("snode", None, None),
        ),
        out_specs=P("snode", None, ("row", "col")),
        check_vma=False,
    )
```

```python
import functools

import jax
import jax.numpy as jnp
from jax import lax
from jax.experimental import pallas as pl
from jax.experimental.pallas import tpu as pltpu
from jax.sharding import PartitionSpec as P

MESH = pl.DeviceIdType.MESH
LANES = 128
PARTS = 4
AWAY = (0, 0, 0, 0, 16, 18, 20, 0)
PICKS = 2


def sizes(row_size, snodes, tile, held, local_rows, local_cols):
    blocks = local_cols // tile
    return dict(
        depth=row_size // 2,
        halves=tile // LANES,
        spans=[(b, 0, tile // PARTS // 2) for b in range(2 * snodes * (tile // LANES))],
        snodes=snodes,
        tile=tile,
        held=held,
        blocks=blocks,
        shares=local_rows // (2 * tile),
        away=[blocks * n // 40 for n in AWAY],
    )


def fused_kernel(cfg, order_hbm, mask_hbm, a_ref, l_ref, d_ref, out_ref, *rest):
    depth, halves, spans = cfg["depth"], cfg["halves"], cfg["spans"]
    phases, buffers = len(spans), spans[-1][0] + 1
    snodes, tile, held = cfg["snodes"], cfg["tile"], cfg["held"]
    blocks, shares, away = cfg["blocks"], cfg["shares"], cfg["away"]
    lanes, rest = rest[:phases], rest[phases:]
    cols, rest = rest[:buffers], rest[buffers:]
    (
        theirs_ref,
        mine_ref,
        d_vm,
        order_vm,
        table_vm,
        inv_ref,
        mask_ref,
        own_ref,
        pick_ref,
        give_ref,
        take_ref,
        res_ref,
        part_ref,
        mine_part_ref,
        b_send,
        c_send,
        y_send,
        x_send,
        o_send,
        b_recv,
        c_recv,
        y_recv,
        x_recv,
        f_recv,
        o_recv,
        a_sem,
        m_sem,
        in_sem,
        out_sem,
    ) = rest
    strip = tile // PARTS // 2
    plane = PARTS * held

    row = lax.axis_index("row")
    y = lax.axis_index("col")
    core = lax.axis_index("snode")
    z = row // 2
    x = row % 2
    me = x * 2 + y
    lane_x = (1 - x) * 2 + y
    lane_y = x * 2 + 1 - y
    lane_d = (1 - x) * 2 + 1 - y
    slot = (row * 2 + y) * held

    def at(zz, xx, yy):
        return (zz * 2 + xx, yy, core)

    sides = [(at(z, 1 - x, y), lane_x), (at(z, x, 1 - y), lane_y), (at(z, 1 - x, 1 - y), lane_d)]
    to_x, to_y = sides[0][0], sides[1][0]
    pair = at(z + 1 - 2 * (z % 2), x, y)
    reach = [dz for dz in (2, -2, 1, -1) if abs(dz) < depth]

    def exists(dz):
        return z + dz < depth if dz > 0 else z + dz >= 0

    inner = jnp.logical_and(z >= 1, z + 1 < depth)
    low = z * 2 < depth
    far = jnp.where(low, z + 2, z - 2)
    near = jnp.where(low, z - 1, z + 1)

    def packed(s):
        return theirs_ref.at[0 : held * tile, s * tile : (s + 1) * tile]

    loads = []
    for s in range(snodes):
        loads.append(pltpu.make_async_copy(l_ref.at[s], packed(s), in_sem.at[s, 0]))
        loads.append(pltpu.make_async_copy(d_ref.at[s], d_vm.at[s], in_sem.at[s, 1]))
    order_load = pltpu.make_async_copy(order_hbm, order_vm, in_sem.at[snodes, 0])
    mask_load = pltpu.make_async_copy(mask_hbm, mask_ref, in_sem.at[snodes, 1])
    table_move = pltpu.make_async_copy(table_vm, inv_ref, in_sem.at[snodes, 0])
    for c in loads[:2] + [order_load] + loads[2:]:
        c.start()

    def theirs_load(i):
        return pltpu.make_async_copy(
            a_ref.at[pl.ds(((1 - y) * shares + i) * tile, tile)],
            theirs_ref.at[pl.ds(i * tile, tile)],
            a_sem.at[i],
        )

    def mine_load(n):
        again = 2 * shares - 1
        i = jnp.where(n < shares, n, jnp.where(n < again, n - shares, n - again))
        return pltpu.make_async_copy(
            a_ref.at[pl.ds((y * shares + i) * tile, tile)], mine_ref.at[n % 2], m_sem.at[n % 2]
        )

    barrier = pltpu.get_barrier_semaphore()
    for dev, _ in sides:
        pl.semaphore_signal(barrier, inc=1, device_id=dev, device_id_type=MESH)
    for dz in reach:

        @pl.when(exists(dz))
        def _():
            pl.semaphore_signal(barrier, inc=1, device_id=at(z + dz, x, y), device_id_type=MESH)

    def normalize(g):
        s, h = g // halves, g % halves
        rows = jnp.dot(
            theirs_ref[0 : held * tile, s * tile : (s + 1) * tile],
            d_vm[s, :, h * LANES : (h + 1) * LANES], preferred_element_type=jnp.float32
        ).reshape(held, PARTS, 2, strip, LANES)
        for u in range(2):
            own_ref[2 * g + u] = rows[:, :, u].astype(own_ref.dtype).transpose(1, 0, 2, 3)
            for p, (b, at_row, size) in enumerate(spans):
                if b == 2 * g + u:
                    lanes[p][pl.ds(slot, held)] = own_ref[b, me, :, at_row : at_row + size]

    for c in loads[:2]:
        c.wait()
    normalize(0)

    @pl.when(inner)
    def _():
        pl.semaphore_wait(barrier, len(sides) + 3)

    @pl.when(jnp.logical_not(inner))
    def _():
        pl.semaphore_wait(barrier, len(sides) + min(2, depth - 1))

    def remote(src, dst, send, recv, dev):
        return pltpu.make_async_remote_copy(
            src_ref=src, dst_ref=dst, send_sem=send, recv_sem=recv, device_id=dev, device_id_type=MESH
        )

    def guarded(cond, fn):
        if cond is None:
            fn()
        else:
            pl.when(cond)(fn)

    def start(make, cond=None):
        guarded(cond, lambda: make().start())

    def arrive(like, sem):
        pltpu.make_async_copy(like, like, sem).wait()

    def part_of(p):
        b, at_row, size = spans[p]
        return b, slice(at_row, at_row + size)

    def strips(p, lane, span):
        b, part = part_of(p)
        return cols[b].at[lane, span, part]

    def picked(p):
        return pick_ref.at[p % PICKS]

    def b_copy(p, k):
        dev, lane = sides[k]
        b, part = part_of(p)
        return remote(
            own_ref.at[b, lane, :, part], lanes[p].at[pl.ds(slot, held)], b_send, b_recv.at[p], dev
        )

    def spread(p):
        for k in (2, 0, 1):
            start(lambda k=k: b_copy(p, k))

    def far_of(zz):
        return jnp.where(zz * 2 < depth, zz + 2, zz - 2)

    def c_copy(p, source, target, index):
        span = pl.ds(source * plane, plane)
        kind = jnp.where(far_of(target) == source, 1, 0)
        return remote(
            lanes[p].at[span],
            lanes[p].at[span],
            c_send.at[index],
            c_recv.at[p, kind],
            at(target, x, y),
        )

    def climb(p):
        b, part = part_of(p)
        arrive(own_ref.at[b, 0:3, :, part], b_recv.at[p])
        for n, dz in enumerate(reach):
            start(lambda n=n, dz=dz: c_copy(p, z, z + dz, n), exists(dz))

    def far_arrives(p):
        arrive(lanes[p].at[0:plane], c_recv.at[p, 1])

    def relay(p):
        if depth < 4:
            return
        guarded(inner if p == phases - 1 else None, lambda: far_arrives(p))
        start(lambda: c_copy(p, far, near, len(reach)), inner)

    def climbed(p):
        others = depth - 1
        if depth >= 4:
            others -= 1
            if p == phases - 1:
                guarded(jnp.logical_not(inner), lambda: far_arrives(p))
        arrive(lanes[p].at[0 : others * plane], c_recv.at[p, 0])

    def y_copy(p):
        return remote(
            picked(p), strips(p, me, slice(0, blocks)), y_send.at[p % PICKS], y_recv.at[p], to_y
        )

    def pieces(p):
        first, rest = away[p], blocks - 2 * away[p]
        if not first:
            return [(0, 0, blocks)]
        return [(0, blocks - first, first)] + ([(first, first, rest)] if rest else [])

    def x_slot(p, kind):
        before = sum(3 if away[n] else 1 for n in range(p))
        return before + (kind if away[p] else 0)

    def x_copy(p, k, n):
        lane = (me, lane_y)[k]
        even, odd, size = pieces(p)[n]
        span = pl.ds(even + (z % 2) * (odd - even), size)
        sem = x_recv.at[x_slot(p, k if away[p] and n == 0 else 2)]
        return remote(strips(p, lane, span), strips(p, lane, span), x_send.at[k], sem, to_x)

    def cross(p, k):
        for n in range(len(pieces(p))):
            start(lambda n=n: x_copy(p, k, n))

    def f_copy(p, k):
        lane = (lane_x, lane_d)[k]
        span = pl.ds((z % 2) * (blocks - away[p]), away[p])
        sem = f_recv.at[sum(1 for n in range(p) if away[n])]
        return remote(strips(p, lane, span), strips(p, lane, span), x_send.at[k], sem, pair)

    def sort(p, own=True):
        climbed(p)
        if p == 0:
            table_move.wait()
        b, part = part_of(p)
        s = b // (2 * halves)

        if p >= PICKS:
            arrive(picked(p), y_send.at[p % PICKS])

        def pick(j, carry):
            pick_ref[p % PICKS, j] = lanes[p][inv_ref[s, (1 - y) * blocks + j, 0]]
            cols[b][me, j, part] = lanes[p][inv_ref[s, y * blocks + j, 0]]
            return carry

        lax.fori_loop(0, blocks, pick, 0)
        start(lambda: y_copy(p))
        if own:
            cross(p, 0)

    def pass_on(p):
        y_copy(p).wait_recv()
        cross(p, 1)

    def forward(p, k):
        if away[p]:
            arrive(strips(p, 0, slice(0, away[p])), x_recv.at[x_slot(p, k)])
            start(lambda: f_copy(p, k))

    def crossed(p):
        size = blocks - 2 * away[p]
        if size:
            arrive(strips(p, slice(0, 2), slice(0, size)), x_recv.at[x_slot(p, 2)])

    def forwarded(p):
        if away[p]:
            arrive(strips(p, slice(0, 2), slice(0, away[p])), f_copy_sem(p))

    def f_copy_sem(p):
        return f_recv.at[sum(1 for n in range(p) if away[n])]

    def make_table():
        order_load.wait()
        shape = (inv_ref.shape[1], order_hbm.shape[1])
        wanted = lax.broadcasted_iota(jnp.int32, shape, 0)
        packed = lax.broadcasted_iota(jnp.int32, shape, 1)
        for s in range(snodes):
            found = jnp.where(order_vm[s : s + 1, :] == wanted, packed, 0)
            place = jnp.max(found, axis=1, keepdims=True)
            table_vm[s] = jnp.broadcast_to(place, table_vm.shape[1:])
        table_move.start()

    def gate_of(i, j):
        return mask_ref[i, y * blocks + j].astype(jnp.float32).astype(theirs_ref.dtype)

    def gate(lo, hi):
        first = row * 2 * shares + (1 - y) * shares

        def one_row(i, carry):
            arrive(theirs_ref.at[pl.ds(i * tile, tile)], a_sem.at[i])
            rows = pl.ds(pl.multiple_of(i * tile, tile), tile)

            def one(j, carry):
                span = pl.ds(pl.multiple_of(j * tile, tile), tile)
                theirs_ref[rows, span] = theirs_ref[rows, span] * gate_of(first + i, j)
                return carry

            return lax.fori_loop(0, blocks, one, carry)

        lax.fori_loop(lo, hi, one_row, 0)

    step = max(n for n in range(1, 5) if blocks % n == 0)
    wide = max(n for n in range(1, 9) if blocks % n == 0)

    def stacked(strips):
        return jnp.stack(strips, axis=2).transpose(1, 0, 2, 3, 4).reshape(-1, LANES)

    def columns(g, c):
        js = slice(c * step, (c + 1) * step)
        return stacked([cols[2 * g + u][:, js] for u in range(2)])

    def o_copy(g, i):
        return remote(
            give_ref.at[g, i], take_ref.at[g, i], o_send, o_recv.at[g // halves, i], to_y
        )

    def send_block(g, i, total):
        give_ref[g, i] = (-total).T.astype(give_ref.dtype)
        o_copy(g, i).start()

    def theirs(g, lo, hi):
        def block(i, carry):
            rows = pl.ds(pl.multiple_of(i * tile, tile), tile)
            total = jnp.zeros((tile, LANES), jnp.float32)
            for c in range(blocks // step):
                total += jnp.dot(
                    theirs_ref[rows, c * step * tile : (c + 1) * step * tile],
                    columns(g, c),
                    preferred_element_type=jnp.float32,
                )
            send_block(g, i, total)
            return carry

        lax.fori_loop(lo, hi, block, 0)

    def side_dot(groups, side, left_of):
        total = jnp.zeros((tile, len(groups) * LANES), jnp.float32)
        for c in range(blocks // wide):
            left = jnp.concatenate(
                [
                    left_of(j, pl.ds(pl.multiple_of(j * tile + side * LANES, LANES), LANES))
                    for j in range(c * wide, (c + 1) * wide)
                ],
                axis=1,
            )
            right = [
                stacked(
                    [cols[2 * g + u][pl.ds(side * 2, 2), c * wide : (c + 1) * wide] for u in range(2)]
                )
                for g in groups
            ]
            total += jnp.dot(
                left, jnp.concatenate(right, axis=1), preferred_element_type=jnp.float32
            )
        return total

    def theirs_near(groups):
        def block(i, carry):
            rows = pl.ds(pl.multiple_of(i * tile, tile), tile)
            part_ref[rows, : len(groups) * LANES] = side_dot(groups, x, lambda j, span: theirs_ref[rows, span])
            return carry

        lax.fori_loop(0, shares, block, 0)

    def theirs_far(g, n):
        def block(i, carry):
            rows = pl.ds(pl.multiple_of(i * tile, tile), tile)
            total = side_dot([g], 1 - x, lambda j, span: theirs_ref[rows, span])
            send_block(g, i, total + part_ref[rows, n * LANES : (n + 1) * LANES])
            if g == buffers // 2 - 1:

                @pl.when(i + 2 < shares)
                def _():
                    late_load(i).start()

            return carry

        lax.fori_loop(0, shares, block, 0)

    def late_load(i):
        return pltpu.make_async_copy(
            a_ref.at[pl.ds((y * shares + 2 + i) * tile, tile)],
            theirs_ref.at[pl.ds(i * tile, tile)],
            a_sem.at[i],
        )

    def finish(s, i, total):
        total = (-total).T
        rows = pl.ds(pl.multiple_of(i * tile, tile), tile)
        both = pl.ds(s * halves, halves)
        arrive(take_ref.at[both, i], o_recv.at[s, i])
        for h in range(halves):
            span = slice(h * LANES, (h + 1) * LANES)
            res_ref[s, span, rows] = (
                total[span] + take_ref[s * halves + h, i].astype(jnp.float32)
            ).astype(res_ref.dtype)
        pltpu.make_async_copy(
            res_ref.at[s, :, rows], out_ref.at[s, :, rows], out_sem.at[s]
        ).start()

    first_mine = row * 2 * shares + y * shares

    def mine(s, lo, hi):
        def block(i, carry):
            n = i
            mine_load(n).wait()
            total = jnp.zeros((tile, tile), jnp.float32)
            for c in range(blocks // step):
                left = jnp.concatenate(
                    [
                        mine_ref[n % 2, :, j * tile : (j + 1) * tile] * gate_of(first_mine + i, j)
                        for j in range(c * step, (c + 1) * step)
                    ],
                    axis=1,
                )
                right = jnp.concatenate(
                    [columns(s * halves + h, c) for h in range(halves)], axis=1
                )
                total += jnp.dot(left, right, preferred_element_type=jnp.float32)
            mine_load(n + 2).start()
            finish(s, i, total)
            return carry

        lax.fori_loop(lo, hi, block, 0)

    tail = snodes - 1
    tail_groups = [tail * halves + h for h in range(halves)]

    def mine_near(lo, hi):
        def block(i, carry):
            n = shares + i
            mine_load(n).wait()
            rows = pl.ds(pl.multiple_of(i * tile, tile), tile)
            mine_part_ref[rows] = side_dot(
                tail_groups, x, lambda j, span: mine_ref[n % 2, :, span] * gate_of(first_mine + i, j)
            )
            mine_load(n + 2).start()
            return carry

        lax.fori_loop(lo, hi, block, 0)

    def mine_far(lo, hi, late, whole):
        def block(i, carry):
            n = 2 * shares - 1 + i
            if late:
                late_load(i - 2).wait()
                source = theirs_ref.at[pl.ds(pl.multiple_of((i - 2) * tile, tile), tile)]
            else:
                mine_load(n).wait()
                source = mine_ref.at[n % 2]
            rows = pl.ds(pl.multiple_of(i * tile, tile), tile)

            def gated(j, span):
                return source[:, span] * gate_of(first_mine + i, j)

            total = side_dot(tail_groups, 1 - x, gated)
            if whole:
                total += side_dot(tail_groups, x, gated)
            else:
                total += mine_part_ref[rows]
            finish(tail, i, total)
            return carry

        lax.fori_loop(lo, hi, block, 0)

    spread(0)
    mask_load.start()
    for n in range(2):
        mine_load(n).start()
    for c in loads[2:]:
        c.wait()
    for g in range(1, buffers // 2):
        normalize(g)
    for i in range(shares):
        theirs_load(i).start()
    climb(0)
    for p in range(1, phases):
        spread(p)
    make_table()
    relay(0)
    climb(1)
    mask_load.wait()
    gate(0, 2)
    sort(0)
    relay(1)
    climb(2)
    gate(2, 5)
    pass_on(0)
    sort(1)
    relay(2)
    climb(3)
    pass_on(1)
    sort(2)
    relay(3)
    climb(4)
    crossed(0)
    crossed(1)
    pass_on(2)
    sort(3)
    theirs(0, 0, 2)
    relay(4)
    climb(5)
    theirs(0, 2, 4)
    pass_on(3)
    theirs(0, 4, 5)
    sort(4)
    relay(5)
    climb(6)
    crossed(2)
    theirs_near([1])
    pass_on(4)
    sort(5)
    relay(6)
    climb(7)
    crossed(3)
    theirs_far(1, 0)
    pass_on(5)
    sort(6)
    relay(7)
    forward(4, 0)
    forward(4, 1)
    mine(0, 0, 3)
    sort(7, False)
    pass_on(6)
    cross(7, 0)
    forward(5, 0)
    forward(5, 1)
    mine(0, 3, 5)
    forward(6, 0)
    crossed(4)
    crossed(5)
    pass_on(7)
    theirs_near([2, 3])
    forward(6, 1)
    mine_near(0, 2)
    forward(7, 0)
    forwarded(4)
    forwarded(5)
    theirs_far(2, 0)
    forward(7, 1)
    mine_near(2, shares - 1)
    crossed(6)
    crossed(7)
    forwarded(6)
    forwarded(7)
    theirs_far(3, 1)
    mine_far(0, 2, False, False)
    mine_far(2, shares - 1, True, False)
    mine_far(shares - 1, shares, True, True)
    for s in range(snodes):
        pltpu.make_async_copy(res_ref.at[s], out_ref.at[s], out_sem.at[s]).wait()
    arrive(own_ref.at[:, 0:3], b_send)
    for n, dz in enumerate(reach):
        guarded(exists(dz), lambda n=n: arrive(own_ref, c_send.at[n]))
    if depth >= 4:
        guarded(inner, lambda: arrive(own_ref, c_send.at[len(reach)]))
    for k in range(PICKS):
        arrive(pick_ref.at[k], y_send.at[k])
    sent = buffers * strip * LANES // tile
    for k in range(2):
        arrive(theirs_ref.at[0:sent], x_send.at[k])
    arrive(give_ref, o_send)


def fused(order, mask, ancestor_inverse, l_rows, diag_inverse, row_size):
    local_rows, local_cols = ancestor_inverse.shape
    snodes, tile = diag_inverse.shape[:2]
    held = l_rows.shape[1] // tile
    cfg = sizes(row_size, snodes, tile, held, local_rows, local_cols)
    blocks, shares, depth = cfg["blocks"], cfg["shares"], cfg["depth"]
    phases, buffers = len(cfg["spans"]), cfg["spans"][-1][0] + 1
    strip = tile // PARTS // 2
    groups = buffers // 2
    halves = cfg["halves"]
    away = cfg["away"]
    total = order.shape[1]
    half = shares * tile
    kind = ancestor_inverse.dtype
    dma = pltpu.SemaphoreType.DMA
    scratch = [pltpu.VMEM((total, size, LANES), kind) for _, _, size in cfg["spans"]]
    scratch += [pltpu.VMEM((PARTS, blocks, strip, LANES), kind) for _ in range(buffers)]
    scratch += [
        pltpu.VMEM((half, local_cols), kind),
        pltpu.VMEM((2, tile, local_cols), kind),
        pltpu.VMEM(diag_inverse.shape, kind),
        pltpu.VMEM(order.shape, jnp.int32),
        pltpu.VMEM((snodes, total, LANES), jnp.int32),
        pltpu.SMEM((snodes, total, LANES), jnp.int32),
        pltpu.SMEM(mask.shape, jnp.int32),
        pltpu.VMEM((buffers, PARTS, held, strip, LANES), kind),
        pltpu.VMEM((PICKS, blocks, strip, LANES), kind),
        pltpu.VMEM((groups, shares, LANES, tile), kind),
        pltpu.VMEM((groups, shares, LANES, tile), kind),
        pltpu.VMEM((snodes, tile, half), kind),
        pltpu.VMEM((half, halves * LANES), jnp.float32),
        pltpu.VMEM((half, halves * LANES), jnp.float32),
        dma,
        dma((5,)),
        dma((PICKS,)),
        dma((2,)),
        dma,
        dma((phases,)),
        dma((phases, 2)),
        dma((phases,)),
        dma((sum(3 if n else 1 for n in away),)),
        dma((max(1, sum(1 for n in away if n)),)),
        dma((snodes, shares)),
        dma((shares,)),
        dma((2,)),
        dma((snodes + 1, 2)),
        dma((snodes,)),
    ]
    anywhere = pl.BlockSpec(memory_space=pl.ANY)
    return pl.pallas_call(
        functools.partial(fused_kernel, cfg),
        out_shape=jax.ShapeDtypeStruct((snodes, tile, half), kind),
        in_specs=[anywhere] * 5,
        out_specs=anywhere,
        scratch_shapes=scratch,
        compiler_params=pltpu.CompilerParams(
            collective_id=0, has_side_effects=True, vmem_limit_bytes=67043328
        ),
        name="fused",
    )(order, mask, ancestor_inverse, l_rows, diag_inverse)


def fast(ancestor_inverse, fill_mask, block_order, l_rows, diag_inverse):
    return fused(
        block_order, fill_mask, ancestor_inverse, l_rows, diag_inverse, lax.axis_size("row")
    )


def plain(ancestor_inverse, fill_mask, block_order, l_rows, diag_inverse):
    row_index = lax.axis_index("row")
    col_index = lax.axis_index("col")
    local_rows, local_cols = ancestor_inverse.shape
    snode_count, tile_size = diag_inverse.shape[:2]
    block_count = fill_mask.shape[0]
    row_blocks = local_rows // tile_size
    col_blocks = local_cols // tile_size
    normed = jnp.einsum(
        "sxy,syz->sxz", l_rows, diag_inverse, preferred_element_type=jnp.float32
    ).astype(jnp.bfloat16)
    wanted = col_index * col_blocks + jnp.arange(col_blocks, dtype=jnp.int32)
    everything = lax.all_gather(normed, ("row", "col"), axis=1, tiled=True)
    pieces = everything.reshape(snode_count, block_count, tile_size, tile_size)
    selector = (block_order[:, None, :] == wanted[None, :, None]).astype(jnp.bfloat16)
    columns = jnp.einsum(
        "saq,sqxy->saxy", selector, pieces, preferred_element_type=jnp.float32
    ).astype(jnp.bfloat16)
    stacked = columns.transpose(1, 2, 0, 3).reshape(local_cols, snode_count * tile_size)
    tile_gate = lax.dynamic_slice(
        fill_mask, (row_index * row_blocks, col_index * col_blocks), (row_blocks, col_blocks)
    ).astype(jnp.bfloat16)
    masked = (
        ancestor_inverse.reshape(row_blocks, tile_size, col_blocks, tile_size)
        * tile_gate[:, None, :, None]
    ).reshape(local_rows, local_cols)
    share_rows = local_rows // lax.axis_size("col")
    own_rows = lax.psum_scatter(
        (-jnp.dot(masked, stacked, preferred_element_type=jnp.float32)).astype(jnp.bfloat16),
        "col",
        scatter_dimension=0,
        tiled=True,
    ).astype(jnp.float32)
    return (
        own_rows.reshape(share_rows, snode_count, tile_size).transpose(1, 2, 0).astype(jnp.bfloat16)
    )


def per_device(ancestor_inverse, fill_mask, block_order, l_rows, diag_inverse):
    tile = diag_inverse.shape[1]
    col_size = lax.axis_size("col")
    if (
        col_size == 2
        and lax.axis_size("row") in (4, 8)
        and tile == 2 * LANES
        and diag_inverse.shape[0] == 2
        and l_rows.shape[1] * col_size <= ancestor_inverse.shape[0]
        and l_rows.shape[1] % tile == 0
        and ancestor_inverse.shape[0] % (col_size * tile) == 0
    ):
        return fast(ancestor_inverse, fill_mask, block_order, l_rows, diag_inverse)
    return plain(ancestor_inverse, fill_mask, block_order, l_rows, diag_inverse)


def solution(mesh):
    return jax.shard_map(
        per_device,
        mesh=mesh,
        in_specs=(
            P(("snode", "row"), "col"),
            P("snode", None),
            P("snode", None),
            P("snode", ("row", "col"), None),
            P("snode", None, None),
        ),
        out_specs=P("snode", None, ("row", "col")),
        check_vma=False,
    )
```
